32 devices in a mesh: gx: 4 (over z), gy: 8 (over y, x, core).
Axes of the slice: x: 2, y: 2, z: 4, core: 2. Of those that a mesh axis runs over, the one named last changes fastest.
Arguments:
- child_dens: bfloat16 [296, 8192], P(None, ('gx', 'gy')), may hold values from -0.625 to 0.625
- users: int32 [2048], P(('gx', 'gy')), may hold values from 0 to 31
- local_dens: bfloat16 [296, 16384], P(None, ('gx', 'gy')), may hold values from -6 to 6
- live: int32 [32], P(('gx', 'gy')), may hold values from 16 to 128, as said below
- m2l_ops: bfloat16 [296, 2368], replicated, may hold values from -0.125 to 0.125
- m2l_lists: int32 [8, 4096], P(None, ('gx', 'gy')), may hold values from -1 to 143, as said below
- leaf_pos: float32 [3, 131072], P(None, ('gx', 'gy')), may hold values from 0 to 1
- leaf_charge: float32 [4, 131072], P(None, ('gx', 'gy')), may hold values from -0.2 to 0.2
- leaf_nbrs: int32 [4096, 27], P(('gx', 'gy')), may hold values from -1 to 159, as said below
Outputs:
- local_exp: float32 [296, 16384], P(None, ('gx', 'gy'))
- near_pot: float32 [4, 131072], P(None, ('gx', 'gy'))
The draws below stay inside these ranges and needn't reach their ends.
Inputs may be any that keep to these rules, and one draw needn't show every extreme that they name: `live`: at least 16 on every device; some device has exactly 128. `m2l_lists`: entry for target slot k lies in k .. k + 16 or is -1. `leaf_nbrs`: entry for leaf l of a device lies in l .. l + 32 or is -1; the first entry is the leaf itself, l + 16.
All inputs are finite; a program needn't handle non-finite values.
Results may differ from the reference program's by a relative error of at most 0.00071.
Values may be sent and summed in bfloat16 or wider, within the bound.
A program may use at most 128 MiB of HBM per device.

```python
import jax
import jax.numpy as jnp
from jax import lax

P_SIZE = 296
Q = 4
NOFF = 8
OCT_DEV = 128
H = 8
SH_DEV = 1
CH_DEV = 64
LEAF_DEV = 128
NPT = 32
NNB = 27
HL = 16
SHARED = 32
NOCT = 4096
CHILDREN = 2048
LEAVES = 4096
DEVICES = 32


def draw_live(key, part):
    key_base, key_full, key_pick = jax.random.split(jax.random.fold_in(key, 11), 3)
    base = jax.random.randint(key_base, (DEVICES,), OCT_DEV // 8, OCT_DEV // 2 + 1)
    full = jax.random.randint(key_full, (DEVICES,), 0, 16) == 0
    pick = jax.random.randint(key_pick, (), 0, DEVICES)
    full = full | (jnp.arange(DEVICES) == pick)
    return jnp.where(full, OCT_DEV, base).astype(jnp.int32)


def draw_m2l_lists(key, part):
    key_step, key_gap = jax.random.split(jax.random.fold_in(key, 23), 2)
    target = jnp.arange(NOCT, dtype=jnp.int32) % OCT_DEV
    step = jax.random.randint(key_step, (NOFF, NOCT), -H, H + 1)
    source = target[None, :] + H + step
    empty = jax.random.randint(key_gap, (NOFF, NOCT), 0, 8) == 0
    source = jnp.where(empty, -1, source)
    source = source.at[0, 0].set(0)
    source = source.at[0, NOCT - 1].set(OCT_DEV + 2 * H - 1)
    source = source.at[1, 0].set(-1)
    return source.astype(jnp.int32)


def draw_leaf_nbrs(key, part):
    key_step, key_gap = jax.random.split(jax.random.fold_in(key, 37), 2)
    local = jnp.arange(LEAVES, dtype=jnp.int32) % LEAF_DEV
    step = jax.random.randint(key_step, (LEAVES, NNB), -HL, HL + 1)
    source = local[:, None] + HL + step
    empty = jax.random.randint(key_gap, (LEAVES, NNB), 0, 8) == 0
    source = jnp.where(empty, -1, source)
    source = source.at[:, 0].set(local + HL)
    source = source.at[0, 1].set(0)
    source = source.at[LEAVES - 1, 2].set(LEAF_DEV + 2 * HL - 1)
    source = source.at[0, 3].set(-1)
    return source.astype(jnp.int32)


def with_ends(entries, rng, smallest, high):
    longest = entries.shape.index(max(entries.shape))
    spots = []
    for shift in (0, 1):
        where = [jax.random.randint(jax.random.fold_in(rng, axis), (), 0, length) for axis, length in enumerate(entries.shape)]
        where[longest] = (where[longest] + shift) % entries.shape[longest]
        spots.append(tuple(where))
    return entries.at[spots[0]].set(smallest).at[spots[1]].set(high)


def steps_of(rng, shape, pieces, low, largest):
    loudness = 1.0
    for axis_at, blocks in pieces:
        steps = jax.random.uniform(jax.random.fold_in(jax.random.fold_in(rng, 6), axis_at), (blocks,), jnp.float32, low / len(pieces), largest / len(pieces))
        loudness = loudness * jnp.repeat(jnp.exp(steps), shape[axis_at] // blocks).reshape((-1,) + (1,) * (len(shape) - 1 - axis_at))
    return loudness


def gaussian(rng, extent, scale, most, shards=(), held_as=jnp.bfloat16):
    factor_of = steps_of(rng, extent, shards, -0.22, 0.18) if shards else 1.0
    entries = jax.random.normal(rng, extent, jnp.float32) * scale * factor_of
    return jnp.minimum(jnp.maximum(entries, -most), most).astype(held_as)


def setup_inputs(seed: int = 0) -> dict:
    splits = jax.random.split(jax.random.key(seed), 10)
    return {
        "child_dens": gaussian(splits[0], (P_SIZE, CHILDREN * Q), 0.04, 0.625, ((1, 32),)),
        "users": with_ends(jax.random.randint(splits[1], (CHILDREN,), 0, SHARED), jax.random.fold_in(splits[1], 1), 0, SHARED - 1).astype(jnp.int32),
        "local_dens": gaussian(splits[2], (P_SIZE, NOCT * Q), 1.0, 6.0, ((1, 32),)),
        "live": draw_live(jax.random.fold_in(splits[9], 71), 0),
        "m2l_ops": gaussian(splits[4], (P_SIZE, NOFF * P_SIZE), (NOFF * P_SIZE) ** -0.5, 0.125),
        "m2l_lists": draw_m2l_lists(jax.random.fold_in(splits[9], 71), 0),
        "leaf_pos": jnp.clip(1.0 * jax.random.uniform(splits[6], (3, LEAVES * NPT), jnp.float32) ** steps_of(splits[6], (3, LEAVES * NPT), ((1, 32),), -0.2, 0.2), 0.0, 1.0),
        "leaf_charge": gaussian(splits[7], (Q, LEAVES * NPT), 0.03, 0.2, ((1, 32),), jnp.float32),
        "leaf_nbrs": draw_leaf_nbrs(jax.random.fold_in(splits[9], 71), 0),
    }


soften = 0.01

def alive_slots(count):
    slot = jnp.arange(OCT_DEV, dtype=jnp.int32)
    lower = count // 2
    upper = count - lower
    return (slot < lower) | (slot >= OCT_DEV - upper)

def m2l_device(window, ops_blocks, lists):
    span = window.shape[1]
    extended = jnp.concatenate([window, jnp.zeros((window.shape[0], 1, window.shape[2]), jnp.float32)], axis=1)
    index = jnp.where(lists < 0, span, lists).astype(jnp.int32)
    gathered = jnp.take(extended, index, axis=1)
    return jnp.einsum('ioj,jotq->itq', ops_blocks, gathered, precision=lax.Precision.HIGHEST)

def near_device(window, nbrs):
    span = window.shape[1]
    extended = jnp.concatenate([window, jnp.zeros((window.shape[0], 1, window.shape[2]), jnp.float32)], axis=1)
    index = jnp.where(nbrs < 0, span, nbrs).astype(jnp.int32)
    source = jnp.take(extended, index, axis=1)
    source = source.reshape(source.shape[0], source.shape[1], -1)
    target = window[:3, HL:HL + LEAF_DEV, :]
    dist_sq = jnp.zeros((LEAF_DEV, NPT, source.shape[2]), jnp.float32)
    for coord in range(3):
        diff = target[coord][:, :, None] - source[coord][:, None, :]
        dist_sq = dist_sq + diff * diff
    kernel = 1.0 / jnp.sqrt(dist_sq + soften)
    return jnp.einsum('lts,qls->qlt', kernel, source[3:], precision=lax.Precision.HIGHEST)

def reference(child_dens, users, local_dens, live, m2l_ops, m2l_lists, leaf_pos, leaf_charge, leaf_nbrs):
    child_blocks = jnp.transpose(child_dens.reshape(P_SIZE, DEVICES, CH_DEV, Q), (1, 2, 0, 3))
    user_blocks = users.reshape(DEVICES, CH_DEV)

    def add_device(total, item):
        block, targets = item
        part_sum = jax.ops.segment_sum(block.astype(jnp.float32), targets, num_segments=SHARED)
        return (total + part_sum, jnp.float32(0.0))
    shared, unused = lax.scan(add_device, jnp.zeros((SHARED, P_SIZE, Q), jnp.float32), (child_blocks, user_blocks))
    shared = jnp.transpose(shared.reshape(DEVICES, SH_DEV, P_SIZE, Q), (2, 0, 1, 3))
    own = local_dens.astype(jnp.float32).reshape(P_SIZE, DEVICES, OCT_DEV, Q)
    own = own.at[:, :, :SH_DEV, :].add(shared)
    alive = jax.vmap(alive_slots)(live)
    owned = jnp.where(alive[None, :, :, None], own, jnp.float32(0.0)).astype(jnp.bfloat16)
    padded = jnp.pad(owned.astype(jnp.float32).reshape(P_SIZE, NOCT, Q), ((0, 0), (H, H), (0, 0)))
    ops_blocks = m2l_ops.astype(jnp.float32).reshape(P_SIZE, NOFF, P_SIZE)
    lists_dev = jnp.transpose(m2l_lists.reshape(NOFF, DEVICES, OCT_DEV), (1, 0, 2))
    points = jnp.concatenate([leaf_pos, leaf_charge], axis=0).reshape(3 + Q, LEAVES, NPT)
    points_padded = jnp.pad(points, ((0, 0), (HL, HL), (0, 0)))
    nbrs_dev = leaf_nbrs.reshape(DEVICES, LEAF_DEV, NNB)
    ranks = jnp.arange(DEVICES, dtype=jnp.int32)

    def per_device(item):
        rank, lists, nbrs, count = item
        window = lax.dynamic_slice_in_dim(padded, rank * OCT_DEV, OCT_DEV + 2 * H, axis=1)
        expansion = m2l_device(window, ops_blocks, lists)
        keep = alive_slots(count)
        expansion = jnp.where(keep[None, :, None], expansion, jnp.float32(0.0))
        leaves = lax.dynamic_slice_in_dim(points_padded, rank * LEAF_DEV, LEAF_DEV + 2 * HL, axis=1)
        return (expansion, near_device(leaves, nbrs))
    expansions, nears = lax.map(per_device, (ranks, lists_dev, nbrs_dev, live))
    local_exp = jnp.transpose(expansions, (1, 0, 2, 3)).reshape(P_SIZE, NOCT * Q)
    near_pot = jnp.transpose(nears, (1, 0, 2, 3)).reshape(Q, LEAVES * NPT)
    return (local_exp, near_pot)
```

```python
import jax
import jax.numpy as jnp
from jax import lax
from jax.experimental import pallas as pl
from jax.experimental.pallas import tpu as pltpu
from jax.sharding import PartitionSpec as P

Q = 4
NOFF = 8
SH_DEV = 1
NPT = 32
HL = 16
GROUP = 4
BLOCK = 32

soften = 0.01
f32 = jnp.float32
bf16 = jnp.bfloat16


def extended_2(block, sides, width):
    for axis, dim in sides:
        count = lax.axis_size(axis)
        forward = [(i, i + 1) for i in range(count - 1)]
        backward = [(target, source) for source, target in forward]
        low = lax.ppermute(
            lax.slice_in_dim(block, block.shape[dim] - width, None, axis=dim), axis, forward
        )
        high = lax.ppermute(lax.slice_in_dim(block, 0, width, axis=dim), axis, backward)
    return low, high


def partner(value, axis, apart):
    mask = 2**apart
    pairs = [(source, source ^ mask) for source in range(lax.axis_size(axis))]
    return lax.ppermute(value, axis, pairs)


def split3(value):
    first = value.astype(bf16).astype(f32)
    rest = value - first
    second = rest.astype(bf16).astype(f32)
    return first, second, rest - second


def row_ids(shape):
    return lax.broadcasted_iota(jnp.int32, shape, 0)


def lane_ids(shape):
    return lax.broadcasted_iota(jnp.int32, shape, 1)


def with_norm(coords):
    norm = jnp.sum(coords * coords, axis=0, keepdims=True)
    return jnp.where(row_ids(coords.shape) == 3, norm, coords), norm


def source_rows(coords):
    value, _ = with_norm(coords)
    one, two, three = split3(value)
    flat = jnp.where(row_ids(value.shape) < 3, f32(1.0), f32(0.0))
    return jnp.concatenate(
        [one, two, three, one, two, one, flat, jnp.zeros_like(one)], axis=0
    ).astype(bf16)


def target_rows(coords):
    value, norm = with_norm(coords)
    one, two, three = split3(value)
    row = row_ids(value.shape)
    main = jnp.where(row < 3, -2.0 * one, jnp.where(row == 3, f32(1.0), f32(0.0)))
    second = jnp.where(row < 3, -2.0 * two, f32(0.0))
    third = jnp.where(row < 3, -2.0 * three, f32(0.0))
    part = split3(norm + soften)
    flat = jnp.where(
        row == 0,
        part[0],
        jnp.where(row == 1, part[1], jnp.where(row == 2, part[2], f32(0.0))),
    )
    return jnp.concatenate(
        [main, main, main, second, second, third, flat, jnp.zeros_like(one)], axis=0
    ).astype(bf16)


def near_counts(nbrs, counts):
    slots, leaves = nbrs.shape
    groups, eight, reach = counts.shape
    span = GROUP + 2 * HL
    rows = -(-span // 16) * 16
    base = nbrs - lane_ids(nbrs.shape) // GROUP * GROUP
    base = jnp.where(nbrs < 0, -1, base)
    ids = row_ids((rows, leaves))
    total = jnp.zeros((rows, leaves), f32)
    for j in range(slots):
        total = total + jnp.where(ids == base[j : j + 1, :], f32(1.0), f32(0.0))
    wide = groups * eight
    lane = lane_ids((leaves, wide))
    twice = row_ids((leaves, wide)) == lane // 8 * GROUP + lane % GROUP
    doubled = jnp.dot(
        total.astype(bf16), jnp.where(twice, f32(1.0), f32(0.0)).astype(bf16),
        preferred_element_type=f32,
    )
    spread = row_ids((rows, reach)) == lane_ids((rows, reach)) // NPT
    full = lax.dot_general(
        doubled.T.astype(bf16),
        jnp.where(spread, f32(1.0), f32(0.0)).astype(bf16),
        (((1,), (0,)), ((), ())),
        preferred_element_type=f32,
    )
    counts[...] = full.reshape(groups, eight, reach)


def near_group(g, sources, targets, charges, counts, out):
    reach = counts.shape[2]
    size = GROUP * NPT
    start = pl.multiple_of(g * size, size)
    left = targets[pl.ds(start, size), :]
    cnt = counts[g]
    half = row_ids(cnt.shape) < GROUP
    ch = charges[:, pl.ds(start, reach)]
    w = jnp.concatenate(
        [cnt * jnp.where(half, ch[p : p + 1], ch[p + 1 : p + 2]) for p in range(0, Q, 2)],
        axis=0,
    )
    wh = w.astype(bf16)
    wl = (w - wh.astype(f32)).astype(bf16)
    w = jnp.concatenate([wh, wl], axis=0)
    acc = jnp.zeros((size, w.shape[0]), f32)
    nt = (((1,), (1,)), ((), ()))
    for at in range(0, reach, 256):
        width = min(256, reach - at)
        right = sources[:, pl.ds(pl.multiple_of(start + at, size), width)]
        dist = jnp.dot(left, right, preferred_element_type=f32)
        kernel = lax.rsqrt(dist)
        high = kernel.astype(bf16)
        low = (kernel - high.astype(f32)).astype(bf16)
        part = w[:, at : at + width]
        acc = acc + lax.dot_general(high, part, nt, preferred_element_type=f32)
        acc = acc + lax.dot_general(low, part, nt, preferred_element_type=f32)
    flat = acc.T
    rows = Q * GROUP
    flat = flat[:rows] + flat[rows:]
    mine = row_ids(flat.shape) % GROUP == lane_ids(flat.shape) // NPT
    flat = jnp.where(mine, flat, f32(0.0))
    out[:, pl.ds(start, size)] = jnp.sum(flat.reshape(Q, GROUP, size), axis=1)


def near_kernel(
    pos, charge, low, high, nbrs, out, coords, charges, sources, targets, counts
):
    halo = low.shape[1]
    count = pos.shape[1]
    coords[...] = jnp.zeros_like(coords)
    for ref, at in ((low, 0), (high, halo + count)):
        coords[0:3, at : at + halo] = ref[0:3, :]
        charges[:, at : at + halo] = ref[3:, :]
    coords[0:3, halo : halo + count] = pos[...]
    charges[:, halo : halo + count] = charge[...]
    sources[...] = source_rows(coords[...])
    targets[...] = target_rows(coords[:, halo : halo + count]).T
    near_counts(nbrs[...], counts)
    groups = counts.shape[0]

    def step(g, carry):
        near_group(g, sources, targets, charges, counts, out)
        return carry

    lax.fori_loop(0, groups, step, 0)


def near_field(pos, charge, low, high, nbrs):
    count = pos.shape[1]
    halo = low.shape[1]
    leaves = count // NPT
    groups = leaves // GROUP
    span = count + 2 * halo
    reach = (GROUP + 2 * HL) * NPT
    return pl.pallas_call(
        near_kernel,
        out_shape=jax.ShapeDtypeStruct(charge.shape, f32),
        scratch_shapes=[
            pltpu.VMEM((8, span), f32),
            pltpu.VMEM((Q, span), f32),
            pltpu.VMEM((64, span), bf16),
            pltpu.VMEM((count, 64), bf16),
            pltpu.VMEM((groups, 8, reach), f32),
        ],
    )(pos, charge, low, high, nbrs.T)


def alive_lanes(live, slots, shape):
    slot = lane_ids(shape) // Q
    lower = live // 2
    return (slot < lower) | (slot >= slots - (live - lower))


def m2l_gather(window, lists, gathered):
    offsets, slots = lists.shape
    surface = window.shape[0]
    wide = slots * Q
    expand = row_ids((slots, wide)) == lane_ids((slots, wide)) // Q
    place = jnp.dot(
        (lists + 1).astype(f32).astype(bf16),
        jnp.where(expand, f32(1.0), f32(0.0)).astype(bf16),
        preferred_element_type=f32,
    ).astype(jnp.int32)
    place = (place - 1) * Q + lane_ids(place.shape) % Q
    size = BLOCK * Q
    depth = (BLOCK + slots // 8) * Q
    for b in range(slots // BLOCK):
        block = window[:, b * size : b * size + depth]
        ids = row_ids((depth, size)) + b * size
        for o in range(0, offsets, 2):
            pair = []
            for k in (o, o + 1):
                hit = ids == place[k : k + 1, b * size : (b + 1) * size]
                hot = jnp.where(hit, f32(1.0), f32(0.0)).astype(bf16)
                pair.append(jnp.dot(block, hot, preferred_element_type=f32))
            both = jnp.concatenate(pair, axis=0).astype(bf16)
            gathered[o * surface : (o + 2) * surface, b * size : (b + 1) * size] = both


def m2l_kernel(live, owned, low, high, lists, ops, out, window, gathered):
    wide = owned.shape[1]
    rim = low.shape[1]
    slots = wide // Q
    window[:, 0:rim] = low[...]
    window[:, rim : rim + wide] = owned[...]
    window[:, rim + wide :] = high[...]
    m2l_gather(window, lists[...], gathered)
    result = jnp.dot(ops[...], gathered[...], preferred_element_type=f32)
    alive = alive_lanes(live[0], slots, result.shape)
    out[...] = jnp.where(alive, result, f32(0.0))


def m2l(live, owned, low, high, lists, ops):
    surface, wide = owned.shape
    vmem = pl.BlockSpec(memory_space=pltpu.VMEM)
    return pl.pallas_call(
        m2l_kernel,
        out_shape=jax.ShapeDtypeStruct((surface, wide), f32),
        in_specs=[pl.BlockSpec(memory_space=pltpu.SMEM)] + [vmem] * 5,
        scratch_shapes=[
            pltpu.VMEM((surface, wide + 2 * low.shape[1]), bf16),
            pltpu.VMEM((surface * lists.shape[0], wide), bf16),
        ],
    )(live, owned, low, high, lists, ops)


def per_device(
    child_dens, users, local_dens, live, m2l_ops, m2l_lists, leaf_pos, leaf_charge, leaf_nbrs
):
    surface = child_dens.shape[0]
    slots = local_dens.shape[1] // Q
    shared_total = SH_DEV * lax.axis_size("gx") * lax.axis_size("gy")
    halo = HL * NPT
    tail = jnp.concatenate([leaf_pos[:, -halo:], leaf_charge[:, -halo:]], axis=0)
    head = jnp.concatenate([leaf_pos[:, :halo], leaf_charge[:, :halo]], axis=0)
    low, high = extended_2(jnp.concatenate([head, tail], axis=1), ((("gx", "gy"), 1),), halo)
    near_pot = near_field(leaf_pos, leaf_charge, low, high, leaf_nbrs)
    children = child_dens.reshape(surface, -1, Q)
    onehot = (users[:, None] == jnp.arange(shared_total, dtype=jnp.int32)[None, :]).astype(
        jnp.bfloat16
    )
    partial_value = jnp.einsum("pcq,cs->psq", children, onehot, preferred_element_type=jnp.float32)
    block = partial_value.reshape(surface, shared_total * Q)
    high_rank = lax.axis_index("gx")
    for bit in range(lax.axis_size("gx").bit_length() - 2, -1, -1):
        half = block.shape[1] // 2
        upper = high_rank >> bit & 1 == 1
        keep = jnp.where(upper, block[:, half:], block[:, :half])
        give = jnp.where(upper, block[:, :half], block[:, half:])
        block = keep + partner(give, "gx", bit)
    low_rank = lax.axis_index("gy")
    for bit in range(lax.axis_size("gy").bit_length() - 2, -1, -1):
        half = block.shape[1] // 2
        upper = low_rank >> bit & 1 == 1
        keep = jnp.where(upper, block[:, half:], block[:, :half])
        give = jnp.where(upper, block[:, :half], block[:, half:])
        block = keep + partner(give, "gy", bit)
    first = SH_DEV * Q
    own = local_dens.astype(jnp.float32)
    own = jnp.concatenate([own[:, :first] + block, own[:, first:]], axis=1)
    slot_ids = jnp.arange(slots * Q, dtype=jnp.int32) // Q
    lower = live[0] // 2
    upper_count = live[0] - lower
    alive = (slot_ids < lower) | (slot_ids >= slots - upper_count)
    owned = jnp.where(alive[None, :], own, jnp.float32(0.0)).astype(jnp.bfloat16)
    rim = slots // 16 * Q
    wlow, whigh = extended_2(owned, ((("gx", "gy"), 1),), rim)
    local_exp = m2l(live, owned, wlow, whigh, m2l_lists, m2l_ops)
    return (local_exp, near_pot)


def solution(mesh):
    placed = (
        P(None, ("gx", "gy")),
        P(("gx", "gy")),
        P(None, ("gx", "gy")),
        P(("gx", "gy")),
        P(),
        P(None, ("gx", "gy")),
        P(None, ("gx", "gy")),
        P(None, ("gx", "gy")),
        P(("gx", "gy"), None),
    )
    return jax.shard_map(
        per_device,
        mesh=mesh,
        in_specs=placed,
        out_specs=(P(None, ("gx", "gy")), P(None, ("gx", "gy"))),
        check_vma=False,
    )
```

```python
import functools

import jax
import jax.numpy as jnp
from jax import lax
from jax.experimental import pallas as pl
from jax.experimental.pallas import tpu as pltpu
from jax.sharding import PartitionSpec as P

Q = 4
NOFF = 8
SH_DEV = 1
NPT = 32
HL = 16
GROUP = 4
BLOCK = 32

soften = 0.01
f32 = jnp.float32
bf16 = jnp.bfloat16
MESH = pl.DeviceIdType.MESH


def split3(value):
    first = value.astype(bf16).astype(f32)
    rest = value - first
    second = rest.astype(bf16).astype(f32)
    return first, second, rest - second


def row_ids(shape):
    return lax.broadcasted_iota(jnp.int32, shape, 0)


def lane_ids(shape):
    return lax.broadcasted_iota(jnp.int32, shape, 1)


def with_norm(coords):
    norm = jnp.sum(coords * coords, axis=0, keepdims=True)
    return jnp.where(row_ids(coords.shape) == 3, norm, coords), norm


def source_rows(coords):
    value, _ = with_norm(coords)
    one, two, three = split3(value)
    flat = jnp.where(row_ids(value.shape) < 3, f32(1.0), f32(0.0))
    return jnp.concatenate(
        [one, two, three, one, two, one, flat, jnp.zeros_like(one)], axis=0
    ).astype(bf16)


def target_rows(coords):
    value, norm = with_norm(coords)
    one, two, three = split3(value)
    row = row_ids(value.shape)
    main = jnp.where(row < 3, -2.0 * one, jnp.where(row == 3, f32(1.0), f32(0.0)))
    second = jnp.where(row < 3, -2.0 * two, f32(0.0))
    third = jnp.where(row < 3, -2.0 * three, f32(0.0))
    part = split3(norm + soften)
    flat = jnp.where(
        row == 0,
        part[0],
        jnp.where(row == 1, part[1], jnp.where(row == 2, part[2], f32(0.0))),
    )
    return jnp.concatenate(
        [main, main, main, second, second, third, flat, jnp.zeros_like(one)], axis=0
    ).astype(bf16)


def near_counts(nbrs, counts):
    slots, leaves = nbrs.shape
    groups, eight, reach = counts.shape
    span = GROUP + 2 * HL
    rows = -(-span // 16) * 16
    base = nbrs - lane_ids(nbrs.shape) // GROUP * GROUP
    base = jnp.where(nbrs < 0, -1, base)
    ids = row_ids((rows, leaves))
    total = jnp.zeros((rows, leaves), f32)
    for j in range(slots):
        total = total + jnp.where(ids == base[j : j + 1, :], f32(1.0), f32(0.0))
    wide = groups * eight
    lane = lane_ids((leaves, wide))
    twice = row_ids((leaves, wide)) == lane // 8 * GROUP + lane % GROUP
    doubled = jnp.dot(
        total.astype(bf16), jnp.where(twice, f32(1.0), f32(0.0)).astype(bf16),
        preferred_element_type=f32,
    )
    spread = row_ids((rows, reach)) == lane_ids((rows, reach)) // NPT
    full = lax.dot_general(
        doubled.T.astype(bf16),
        jnp.where(spread, f32(1.0), f32(0.0)).astype(bf16),
        (((1,), (0,)), ((), ())),
        preferred_element_type=f32,
    )
    counts[...] = full.reshape(groups, eight, reach)


def near_group(g, sources, targets, charges, counts, out):
    reach = counts.shape[2]
    size = GROUP * NPT
    start = pl.multiple_of(g * size, size)
    left = targets[pl.ds(start, size), :]
    cnt = counts[g]
    half = row_ids(cnt.shape) < GROUP
    ch = charges[:, pl.ds(start, reach)]
    w = jnp.concatenate(
        [cnt * jnp.where(half, ch[p : p + 1], ch[p + 1 : p + 2]) for p in range(0, Q, 2)],
        axis=0,
    )
    wh = w.astype(bf16)
    wl = (w - wh.astype(f32)).astype(bf16)
    w = jnp.concatenate([wh, wl], axis=0)
    acc = jnp.zeros((size, w.shape[0]), f32)
    nt = (((1,), (1,)), ((), ()))
    for at in range(0, reach, 256):
        width = min(256, reach - at)
        right = sources[:, pl.ds(pl.multiple_of(start + at, size), width)]
        dist = jnp.dot(left, right, preferred_element_type=f32)
        kernel = lax.rsqrt(dist)
        high = kernel.astype(bf16)
        low = (kernel - high.astype(f32)).astype(bf16)
        part = w[:, at : at + width]
        acc = acc + lax.dot_general(high, part, nt, preferred_element_type=f32)
        acc = acc + lax.dot_general(low, part, nt, preferred_element_type=f32)
    flat = acc.T
    rows = Q * GROUP
    flat = flat[:rows] + flat[rows:]
    mine = row_ids(flat.shape) % GROUP == lane_ids(flat.shape) // NPT
    flat = jnp.where(mine, flat, f32(0.0))
    out[:, pl.ds(start, size)] = jnp.sum(flat.reshape(Q, GROUP, size), axis=1)


def alive_lanes(live, slots, shape):
    slot = lane_ids(shape) // Q
    lower = live // 2
    return (slot < lower) | (slot >= slots - (live - lower))


def m2l_gather(window, lists, gathered):
    offsets, slots = lists.shape
    surface = window.shape[0]
    wide = slots * Q
    expand = row_ids((slots, wide)) == lane_ids((slots, wide)) // Q
    place = jnp.dot(
        (lists + 1).astype(f32).astype(bf16),
        jnp.where(expand, f32(1.0), f32(0.0)).astype(bf16),
        preferred_element_type=f32,
    ).astype(jnp.int32)
    place = (place - 1) * Q + lane_ids(place.shape) % Q
    size = BLOCK * Q
    depth = (BLOCK + slots // 8) * Q
    for b in range(slots // BLOCK):
        block = window[:, b * size : b * size + depth]
        ids = row_ids((depth, size)) + b * size
        for o in range(0, offsets, 2):
            pair = []
            for k in (o, o + 1):
                hit = ids == place[k : k + 1, b * size : (b + 1) * size]
                hot = jnp.where(hit, f32(1.0), f32(0.0)).astype(bf16)
                pair.append(jnp.dot(block, hot, preferred_element_type=f32))
            both = jnp.concatenate(pair, axis=0).astype(bf16)
            gathered[o * surface : (o + 2) * surface, b * size : (b + 1) * size] = both


def partial_sums(child, users, send, nx, ny):
    own = SH_DEV * Q
    rows = send.shape[0]
    chunks, count = users.shape
    wide = count * Q
    row = row_ids((rows, wide))
    owner = row // own % nx * ny + row // (own * nx)
    target = owner * own + row % own
    expand = row_ids((count, wide)) == lane_ids((count, wide)) // Q
    expand = jnp.where(expand, f32(1.0), f32(0.0)).astype(bf16)

    def chunk_sum(i):
        ids = users[pl.ds(i, 1), :]
        both = jnp.concatenate([ids // 256, ids % 256], axis=0)
        both = jnp.concatenate([both, both, both, both], axis=0)
        place = jnp.dot(
            both.astype(f32).astype(bf16), expand, preferred_element_type=f32
        ).astype(jnp.int32)
        place = (place[0:1] * 256 + place[1:2]) * Q + lane_ids((1, wide)) % Q
        hot = jnp.where(target == place, f32(1.0), f32(0.0)).astype(bf16)
        block = child[:, pl.ds(pl.multiple_of(i * wide, wide), wide)]
        return lax.dot_general(
            hot, block, (((1,), (1,)), ((), ())), preferred_element_type=f32
        )

    send[...] = chunk_sum(0)
    if chunks > 1:

        def step(i, carry):
            send[...] += chunk_sum(i)
            return carry

        lax.fori_loop(1, chunks, step, 0)


def fused_kernel(
    nx,
    ny,
    live,
    child,
    users,
    local,
    pos,
    charge,
    nbrs,
    window,
    out,
    send1,
    recv1,
    send2,
    recv2,
    spread,
    first,
    last,
    low,
    high,
    pos_low,
    pos_high,
    charge_low,
    charge_high,
    coords,
    charges,
    sources,
    targets,
    counts,
    send_sem,
    recv_sem,
):
    mx, my = lax.axis_index("gx"), lax.axis_index("gy")
    total = nx * ny
    me = mx * ny + my
    after, before = lax.rem(me + 1, total), lax.rem(me + total - 1, total)
    after = (after // ny, lax.rem(after, ny))
    before = (before // ny, lax.rem(before, ny))
    along_y = [(mx, lax.rem(my + d, ny)) for d in range(1, ny)]
    along_x = [(lax.rem(mx + d, nx), my) for d in range(1, nx)]

    barrier = pltpu.get_barrier_semaphore()
    for device in along_y + along_x + [after, before]:
        pl.semaphore_signal(barrier, inc=1, device_id=device, device_id_type=MESH)

    surface, wide = local.shape
    slots = wide // Q
    rim = low.shape[1]
    halo = pos_low.shape[1]
    count = pos.shape[1]
    own = SH_DEV * Q
    message = nx * own
    partial_sums(child, users, send1, nx, ny)
    alive = alive_lanes(live[0], slots, (surface, wide))
    owned = jnp.where(alive, local[...].astype(f32), f32(0.0)).astype(bf16)
    last[...] = owned[:, wide - rim :]
    pl.semaphore_wait(barrier, len(along_y) + len(along_x) + 2)

    at = [0]

    def remote(src, dst, device):
        k = at[0]
        at[0] += 1
        copy = pltpu.make_async_remote_copy(
            src_ref=src,
            dst_ref=dst,
            send_sem=send_sem.at[k],
            recv_sem=recv_sem.at[k],
            device_id=device,
            device_id_type=MESH,
        )
        copy.start()
        return copy

    step1 = []
    for d in range(1, ny):
        start = pl.multiple_of(lax.rem(my + d, ny) * message, message)
        step1.append(
            remote(send1.at[pl.ds(start, message), :], recv1.at[d - 1], along_y[d - 1])
        )
    leaf = [
        remote(pos.at[:, count - halo : count], pos_low, after),
        remote(charge.at[:, count - halo : count], charge_low, after),
        remote(pos.at[:, 0:halo], pos_high, before),
        remote(charge.at[:, 0:halo], charge_high, before),
    ]
    rims = [remote(last, low, after)]

    coords[...] = jnp.zeros_like(coords)
    coords[0:3, halo : halo + count] = pos[...]
    charges[:, halo : halo + count] = charge[...]
    mine = coords[:, halo : halo + count]
    sources[:, halo : halo + count] = source_rows(mine)
    targets[...] = target_rows(mine).T
    near_counts(nbrs[...], counts)
    groups = counts.shape[0]
    skip = halo // (GROUP * NPT)

    def step(g, carry):
        near_group(g, sources, targets, charges, counts, out)
        return carry

    third = (groups - 2 * skip) // 3
    lax.fori_loop(skip, skip + third, step, 0)

    for copy in step1:
        copy.wait()
    value = send1[pl.ds(pl.multiple_of(my * message, message), message), :]
    for d in range(ny - 1):
        value = value + recv1[d]
    for k in range(nx):
        send2[k] = value[k * own : (k + 1) * own]
    step2 = []
    for d in range(1, nx):
        step2.append(remote(send2.at[lax.rem(mx + d, nx)], recv2.at[d - 1], along_x[d - 1]))

    lax.fori_loop(skip + third, skip + 2 * third, step, 0)

    for copy in step2:
        copy.wait()
    shared = send2[mx]
    for d in range(nx - 1):
        shared = shared + recv2[d]
    spread[...] = jnp.zeros_like(spread)
    spread[0:own, :] = shared
    lanes = spread.shape[0]
    front = local[:, 0:lanes].astype(f32) + spread[...].T
    front = jnp.where(alive[:, 0:lanes], front, f32(0.0)).astype(bf16)
    first[...] = front[:, 0:rim]
    rims.append(remote(first, high, before))
    window[:, rim : rim + lanes] = front
    window[:, rim + lanes : rim + wide] = owned[:, lanes:]

    lax.fori_loop(skip + 2 * third, groups - skip, step, 0)

    for copy in leaf:
        copy.wait()
    has_low = me > 0
    has_high = me < total - 1
    for pos_ref, charge_ref, start, there in (
        (pos_low, charge_low, 0, has_low),
        (pos_high, charge_high, halo + count, has_high),
    ):
        span = slice(start, start + halo)
        coords[0:3, span] = pos_ref[...]
        charges[:, span] = jnp.where(there, charge_ref[...], f32(0.0))
        sources[:, span] = source_rows(coords[:, span])
    lax.fori_loop(0, skip, step, 0)
    lax.fori_loop(groups - skip, groups, step, 0)

    for copy in rims:
        copy.wait()
    window[:, 0:rim] = jnp.where(has_low, low[...], jnp.zeros_like(low))
    window[:, rim + wide :] = jnp.where(has_high, high[...], jnp.zeros_like(high))


def fused(live, child, users, local, pos, charge, nbrs):
    nx, ny = lax.axis_size("gx"), lax.axis_size("gy")
    surface, wide = local.shape
    count = pos.shape[1]
    halo = HL * NPT
    groups = count // NPT // GROUP
    span = count + 2 * halo
    reach = (GROUP + 2 * HL) * NPT
    rim = wide // 16
    own = SH_DEV * Q
    copies = ny - 1 + nx - 1 + 6
    vmem = pl.BlockSpec(memory_space=pltpu.VMEM)
    return pl.pallas_call(
        functools.partial(fused_kernel, nx, ny),
        out_shape=(
            jax.ShapeDtypeStruct((surface, wide + 2 * rim), bf16),
            jax.ShapeDtypeStruct(charge.shape, f32),
        ),
        in_specs=[pl.BlockSpec(memory_space=pltpu.SMEM)] + [vmem] * 6,
        out_specs=(vmem, vmem),
        scratch_shapes=[
            pltpu.VMEM((ny * nx * own, surface), f32),
            pltpu.VMEM((ny - 1, nx * own, surface), f32),
            pltpu.VMEM((nx, own, surface), f32),
            pltpu.VMEM((nx - 1, own, surface), f32),
            pltpu.VMEM((128, surface), f32),
            pltpu.VMEM((surface, rim), bf16),
            pltpu.VMEM((surface, rim), bf16),
            pltpu.VMEM((surface, rim), bf16),
            pltpu.VMEM((surface, rim), bf16),
            pltpu.VMEM((3, halo), f32),
            pltpu.VMEM((3, halo), f32),
            pltpu.VMEM((Q, halo), f32),
            pltpu.VMEM((Q, halo), f32),
            pltpu.VMEM((8, span), f32),
            pltpu.VMEM((Q, span), f32),
            pltpu.VMEM((64, span), bf16),
            pltpu.VMEM((count, 64), bf16),
            pltpu.VMEM((groups, 8, reach), f32),
            pltpu.SemaphoreType.DMA((copies,)),
            pltpu.SemaphoreType.DMA((copies,)),
        ],
        compiler_params=pltpu.CompilerParams(collective_id=0, has_side_effects=True),
    )(live, child, users.reshape(-1, 64), local, pos, charge, nbrs.T)


def m2l_kernel(live, window, lists, ops, out, gathered):
    m2l_gather(window, lists[...], gathered)
    result = jnp.dot(ops[...], gathered[...], preferred_element_type=f32)
    alive = alive_lanes(live[0], lists.shape[1], result.shape)
    out[...] = jnp.where(alive, result, f32(0.0))


def m2l(live, window, lists, ops):
    surface = window.shape[0]
    wide = lists.shape[1] * Q
    vmem = pl.BlockSpec(memory_space=pltpu.VMEM)
    return pl.pallas_call(
        m2l_kernel,
        out_shape=jax.ShapeDtypeStruct((surface, wide), f32),
        in_specs=[pl.BlockSpec(memory_space=pltpu.SMEM)] + [vmem] * 3,
        scratch_shapes=[pltpu.VMEM((surface * lists.shape[0], wide), bf16)],
    )(live, window, lists, ops)


def per_device(
    child_dens, users, local_dens, live, m2l_ops, m2l_lists, leaf_pos, leaf_charge, leaf_nbrs
):
    window, near_pot = fused(
        live, child_dens, users, local_dens, leaf_pos, leaf_charge, leaf_nbrs
    )
    return (m2l(live, window, m2l_lists, m2l_ops), near_pot)


def solution(mesh):
    placed = (
        P(None, ("gx", "gy")),
        P(("gx", "gy")),
        P(None, ("gx", "gy")),
        P(("gx", "gy")),
        P(),
        P(None, ("gx", "gy")),
        P(None, ("gx", "gy")),
        P(None, ("gx", "gy")),
        P(("gx", "gy"), None),
    )
    return jax.shard_map(
        per_device,
        mesh=mesh,
        in_specs=placed,
        out_specs=(P(None, ("gx", "gy")), P(None, ("gx", "gy"))),
        check_vma=False,
    )
```

```python
import functools

import jax
import jax.numpy as jnp
from jax import lax
from jax.experimental import pallas as pl
from jax.experimental.pallas import tpu as pltpu
from jax.sharding import PartitionSpec as P

Q = 4
NOFF = 8
SH_DEV = 1
NPT = 32
HL = 16
GROUP = 8
BLOCK = 32

soften = 0.01
f32 = jnp.float32
bf16 = jnp.bfloat16
MESH = pl.DeviceIdType.MESH


def split3(value):
    first = value.astype(bf16).astype(f32)
    rest = value - first
    second = rest.astype(bf16).astype(f32)
    return first, second, rest - second


def row_ids(shape):
    return lax.broadcasted_iota(jnp.int32, shape, 0)


def lane_ids(shape):
    return lax.broadcasted_iota(jnp.int32, shape, 1)


def with_norm(coords):
    norm = jnp.sum(coords * coords, axis=0, keepdims=True)
    return jnp.where(row_ids(coords.shape) == 3, norm, coords), norm


def source_rows(coords):
    value, _ = with_norm(coords)
    one, two, three = split3(value)
    flat = jnp.where(row_ids(value.shape) < 3, f32(1.0), f32(0.0))
    return jnp.concatenate(
        [one, two, three, one, two, one, flat, jnp.zeros_like(one)], axis=0
    ).astype(bf16)


def target_rows(coords):
    value, norm = with_norm(coords)
    one, two, three = split3(value)
    row = row_ids(value.shape)
    main = jnp.where(row < 3, -2.0 * one, jnp.where(row == 3, f32(1.0), f32(0.0)))
    second = jnp.where(row < 3, -2.0 * two, f32(0.0))
    third = jnp.where(row < 3, -2.0 * three, f32(0.0))
    part = split3(norm + soften)
    flat = jnp.where(
        row == 0,
        part[0],
        jnp.where(row == 1, part[1], jnp.where(row == 2, part[2], f32(0.0))),
    )
    return jnp.concatenate(
        [main, main, main, second, second, third, flat, jnp.zeros_like(one)], axis=0
    ).astype(bf16)


def near_counts(nbrs, counts):
    slots, leaves = nbrs.shape
    groups, eight, reach = counts.shape
    span = GROUP + 2 * HL
    rows = -(-span // 16) * 16
    base = nbrs - lane_ids(nbrs.shape) // GROUP * GROUP
    base = jnp.where(nbrs < 0, -1, base)
    ids = row_ids((rows, leaves))
    total = jnp.zeros((rows, leaves), f32)
    for j in range(slots):
        total = total + jnp.where(ids == base[j : j + 1, :], f32(1.0), f32(0.0))
    spread = row_ids((rows, reach)) == lane_ids((rows, reach)) // NPT
    full = lax.dot_general(
        total.T.astype(bf16),
        jnp.where(spread, f32(1.0), f32(0.0)).astype(bf16),
        (((1,), (0,)), ((), ())),
        preferred_element_type=f32,
    )
    counts[...] = full.reshape(groups, eight, reach)


def near_group(g, sources, targets, charges, counts, out):
    reach = counts.shape[2]
    size = GROUP * NPT
    rows = Q * GROUP
    start = pl.multiple_of(g * size, size)
    right = targets[:, pl.ds(start, size)]
    cnt = counts[g]
    ch = charges[:, pl.ds(start, reach)]
    w = jnp.concatenate([cnt * ch[q : q + 1] for q in range(Q)], axis=0)
    wh = w.astype(bf16)
    wl = (w - wh.astype(f32)).astype(bf16)
    w = jnp.concatenate([wh, wl], axis=0)
    total = jnp.zeros((2 * rows, size), f32)
    extra = jnp.zeros((rows, size), f32)
    for at in range(0, reach, 256):
        width = min(256, reach - at)
        left = sources[pl.ds(pl.multiple_of(start + at, size), width), :]
        kernel = lax.rsqrt(jnp.dot(left, right, preferred_element_type=f32))
        high = kernel.astype(bf16)
        low = (kernel - high.astype(f32)).astype(bf16)
        span = slice(at, at + width)
        total = total + jnp.dot(w[:, span], high, preferred_element_type=f32)
        extra = extra + jnp.dot(wh[:, span], low, preferred_element_type=f32)
    flat = total[:rows] + total[rows:] + extra
    mine = row_ids(flat.shape) % GROUP == lane_ids(flat.shape) // NPT
    flat = jnp.where(mine, flat, f32(0.0))
    out[:, pl.ds(start, size)] = jnp.sum(flat.reshape(Q, GROUP, size), axis=1)


def alive_lanes(live, slots, shape):
    slot = lane_ids(shape) // Q
    lower = live // 2
    return (slot < lower) | (slot >= slots - (live - lower))


def m2l_gather(window, lists, gathered):
    offsets, slots = lists.shape
    surface = window.shape[0]
    wide = slots * Q
    expand = row_ids((slots, wide)) == lane_ids((slots, wide)) // Q
    place = jnp.dot(
        (lists + 1).astype(f32).astype(bf16),
        jnp.where(expand, f32(1.0), f32(0.0)).astype(bf16),
        preferred_element_type=f32,
    ).astype(jnp.int32)
    place = (place - 1) * Q + lane_ids(place.shape) % Q
    size = BLOCK * Q
    depth = (BLOCK + slots // 8) * Q
    for b in range(slots // BLOCK):
        block = window[:, b * size : b * size + depth]
        ids = row_ids((depth, size)) + b * size
        for o in range(0, offsets, 2):
            pair = []
            for k in (o, o + 1):
                hit = ids == place[k : k + 1, b * size : (b + 1) * size]
                hot = jnp.where(hit, f32(1.0), f32(0.0)).astype(bf16)
                pair.append(jnp.dot(block, hot, preferred_element_type=f32))
            both = jnp.concatenate(pair, axis=0).astype(bf16)
            gathered[o * surface : (o + 2) * surface, b * size : (b + 1) * size] = both


def partial_sums(child, users, send, nx, ny):
    own = SH_DEV * Q
    rows = send.shape[0]
    chunks, count = users.shape
    wide = count * Q
    row = row_ids((rows, wide))
    owner = row // own % nx * ny + row // (own * nx)
    target = owner * own + row % own
    expand = row_ids((count, wide)) == lane_ids((count, wide)) // Q
    expand = jnp.where(expand, f32(1.0), f32(0.0)).astype(bf16)

    def chunk_sum(i):
        ids = users[pl.ds(i, 1), :]
        both = jnp.concatenate([ids // 256, ids % 256], axis=0)
        both = jnp.concatenate([both, both, both, both], axis=0)
        place = jnp.dot(
            both.astype(f32).astype(bf16), expand, preferred_element_type=f32
        ).astype(jnp.int32)
        place = (place[0:1] * 256 + place[1:2]) * Q + lane_ids((1, wide)) % Q
        hot = jnp.where(target == place, f32(1.0), f32(0.0)).astype(bf16)
        block = child[:, pl.ds(pl.multiple_of(i * wide, wide), wide)]
        return lax.dot_general(
            hot, block, (((1,), (1,)), ((), ())), preferred_element_type=f32
        )

    send[...] = chunk_sum(0)
    if chunks > 1:

        def step(i, carry):
            send[...] += chunk_sum(i)
            return carry

        lax.fori_loop(1, chunks, step, 0)


def fused_kernel(
    nx,
    ny,
    live,
    child,
    users,
    local,
    pos,
    charge,
    nbrs,
    window,
    out,
    send1,
    recv1,
    send2,
    recv2,
    spread,
    first,
    last,
    low,
    high,
    pos_low,
    pos_high,
    charge_low,
    charge_high,
    coords,
    charges,
    sources,
    targets,
    counts,
    send_sem,
    recv_sem,
):
    mx, my = lax.axis_index("gx"), lax.axis_index("gy")
    total = nx * ny
    me = mx * ny + my
    after, before = lax.rem(me + 1, total), lax.rem(me + total - 1, total)
    after = (after // ny, lax.rem(after, ny))
    before = (before // ny, lax.rem(before, ny))
    along_y = [(mx, lax.rem(my + d, ny)) for d in range(1, ny)]
    along_x = [(lax.rem(mx + d, nx), my) for d in range(1, nx)]

    barrier = pltpu.get_barrier_semaphore()
    for device in along_y + along_x + [after, before]:
        pl.semaphore_signal(barrier, inc=1, device_id=device, device_id_type=MESH)

    surface, wide = local.shape
    slots = wide // Q
    rim = low.shape[1]
    halo = pos_low.shape[1]
    count = pos.shape[1]
    own = SH_DEV * Q
    message = nx * own
    partial_sums(child, users, send1, nx, ny)
    alive = alive_lanes(live[0], slots, (surface, wide))
    owned = jnp.where(alive, local[...].astype(f32), f32(0.0)).astype(bf16)
    last[...] = owned[:, wide - rim :]
    pl.semaphore_wait(barrier, len(along_y) + len(along_x) + 2)

    at = [0]

    def remote(src, dst, device):
        k = at[0]
        at[0] += 1
        copy = pltpu.make_async_remote_copy(
            src_ref=src,
            dst_ref=dst,
            send_sem=send_sem.at[k],
            recv_sem=recv_sem.at[k],
            device_id=device,
            device_id_type=MESH,
        )
        copy.start()
        return copy

    step1 = []
    for d in range(1, ny):
        start = pl.multiple_of(lax.rem(my + d, ny) * message, message)
        step1.append(
            remote(send1.at[pl.ds(start, message), :], recv1.at[d - 1], along_y[d - 1])
        )
    leaf = [
        remote(pos.at[:, count - halo : count], pos_low, after),
        remote(charge.at[:, count - halo : count], charge_low, after),
        remote(pos.at[:, 0:halo], pos_high, before),
        remote(charge.at[:, 0:halo], charge_high, before),
    ]
    rims = [remote(last, low, after)]

    coords[...] = jnp.zeros_like(coords)
    coords[0:3, halo : halo + count] = pos[...]
    charges[:, halo : halo + count] = charge[...]
    mine = coords[:, halo : halo + count]
    sources[halo : halo + count, :] = source_rows(mine).T
    targets[...] = target_rows(mine)
    near_counts(nbrs[...], counts)
    groups = counts.shape[0]
    skip = halo // (GROUP * NPT)

    def step(g, carry):
        near_group(g, sources, targets, charges, counts, out)
        return carry

    third = (groups - 2 * skip) // 3
    lax.fori_loop(skip, skip + third, step, 0)

    for copy in step1:
        copy.wait()
    value = send1[pl.ds(pl.multiple_of(my * message, message), message), :]
    for d in range(ny - 1):
        value = value + recv1[d]
    for k in range(nx):
        send2[k] = value[k * own : (k + 1) * own]
    step2 = []
    for d in range(1, nx):
        step2.append(remote(send2.at[lax.rem(mx + d, nx)], recv2.at[d - 1], along_x[d - 1]))

    lax.fori_loop(skip + third, skip + 2 * third, step, 0)

    for copy in step2:
        copy.wait()
    shared = send2[mx]
    for d in range(nx - 1):
        shared = shared + recv2[d]
    spread[...] = jnp.zeros_like(spread)
    spread[0:own, :] = shared
    lanes = spread.shape[0]
    front = local[:, 0:lanes].astype(f32) + spread[...].T
    front = jnp.where(alive[:, 0:lanes], front, f32(0.0)).astype(bf16)
    first[...] = front[:, 0:rim]
    rims.append(remote(first, high, before))
    window[:, rim : rim + lanes] = front
    window[:, rim + lanes : rim + wide] = owned[:, lanes:]

    lax.fori_loop(skip + 2 * third, groups - skip, step, 0)

    for copy in leaf:
        copy.wait()
    has_low = me > 0
    has_high = me < total - 1
    for pos_ref, charge_ref, start, there in (
        (pos_low, charge_low, 0, has_low),
        (pos_high, charge_high, halo + count, has_high),
    ):
        span = slice(start, start + halo)
        coords[0:3, span] = pos_ref[...]
        charges[:, span] = jnp.where(there, charge_ref[...], f32(0.0))
        sources[span, :] = source_rows(coords[:, span]).T
    lax.fori_loop(0, skip, step, 0)
    lax.fori_loop(groups - skip, groups, step, 0)

    for copy in rims:
        copy.wait()
    window[:, 0:rim] = jnp.where(has_low, low[...], jnp.zeros_like(low))
    window[:, rim + wide :] = jnp.where(has_high, high[...], jnp.zeros_like(high))


def fused(live, child, users, local, pos, charge, nbrs):
    nx, ny = lax.axis_size("gx"), lax.axis_size("gy")
    surface, wide = local.shape
    count = pos.shape[1]
    halo = HL * NPT
    groups = count // NPT // GROUP
    span = count + 2 * halo
    reach = (GROUP + 2 * HL) * NPT
    rim = wide // 16
    own = SH_DEV * Q
    copies = ny - 1 + nx - 1 + 6
    vmem = pl.BlockSpec(memory_space=pltpu.VMEM)
    return pl.pallas_call(
        functools.partial(fused_kernel, nx, ny),
        out_shape=(
            jax.ShapeDtypeStruct((surface, wide + 2 * rim), bf16),
            jax.ShapeDtypeStruct(charge.shape, f32),
        ),
        in_specs=[pl.BlockSpec(memory_space=pltpu.SMEM)] + [vmem] * 6,
        out_specs=(vmem, vmem),
        scratch_shapes=[
            pltpu.VMEM((ny * nx * own, surface), f32),
            pltpu.VMEM((ny - 1, nx * own, surface), f32),
            pltpu.VMEM((nx, own, surface), f32),
            pltpu.VMEM((nx - 1, own, surface), f32),
            pltpu.VMEM((128, surface), f32),
            pltpu.VMEM((surface, rim), bf16),
            pltpu.VMEM((surface, rim), bf16),
            pltpu.VMEM((surface, rim), bf16),
            pltpu.VMEM((surface, rim), bf16),
            pltpu.VMEM((3, halo), f32),
            pltpu.VMEM((3, halo), f32),
            pltpu.VMEM((Q, halo), f32),
            pltpu.VMEM((Q, halo), f32),
            pltpu.VMEM((8, span), f32),
            pltpu.VMEM((Q, span), f32),
            pltpu.VMEM((span, 64), bf16),
            pltpu.VMEM((64, count), bf16),
            pltpu.VMEM((groups, GROUP, reach), f32),
            pltpu.SemaphoreType.DMA((copies,)),
            pltpu.SemaphoreType.DMA((copies,)),
        ],
        compiler_params=pltpu.CompilerParams(collective_id=0, has_side_effects=True),
    )(live, child, users.reshape(-1, 64), local, pos, charge, nbrs.T)


def m2l_kernel(live, window, lists, ops, out, gathered):
    m2l_gather(window, lists[...], gathered)
    result = jnp.dot(ops[...], gathered[...], preferred_element_type=f32)
    alive = alive_lanes(live[0], lists.shape[1], result.shape)
    out[...] = jnp.where(alive, result, f32(0.0))


def m2l(live, window, lists, ops):
    surface = window.shape[0]
    wide = lists.shape[1] * Q
    vmem = pl.BlockSpec(memory_space=pltpu.VMEM)
    return pl.pallas_call(
        m2l_kernel,
        out_shape=jax.ShapeDtypeStruct((surface, wide), f32),
        in_specs=[pl.BlockSpec(memory_space=pltpu.SMEM)] + [vmem] * 3,
        scratch_shapes=[pltpu.VMEM((surface * lists.shape[0], wide), bf16)],
    )(live, window, lists, ops)


def per_device(
    child_dens, users, local_dens, live, m2l_ops, m2l_lists, leaf_pos, leaf_charge, leaf_nbrs
):
    window, near_pot = fused(
        live, child_dens, users, local_dens, leaf_pos, leaf_charge, leaf_nbrs
    )
    return (m2l(live, window, m2l_lists, m2l_ops), near_pot)


def solution(mesh):
    placed = (
        P(None, ("gx", "gy")),
        P(("gx", "gy")),
        P(None, ("gx", "gy")),
        P(("gx", "gy")),
        P(),
        P(None, ("gx", "gy")),
        P(None, ("gx", "gy")),
        P(None, ("gx", "gy")),
        P(("gx", "gy"), None),
    )
    return jax.shard_map(
        per_device,
        mesh=mesh,
        in_specs=placed,
        out_specs=(P(None, ("gx", "gy")), P(None, ("gx", "gy"))),
        check_vma=False,
    )
```

```python
import functools

import jax
import jax.numpy as jnp
from jax import lax
from jax.experimental import pallas as pl
from jax.experimental.pallas import tpu as pltpu
from jax.sharding import PartitionSpec as P

Q = 4
NOFF = 8
SH_DEV = 1
NPT = 32
HL = 16
GROUP = 8
BLOCK = 32

soften = 0.01
f32 = jnp.float32
bf16 = jnp.bfloat16
MESH = pl.DeviceIdType.MESH


def split3(value):
    first = value.astype(bf16).astype(f32)
    rest = value - first
    second = rest.astype(bf16).astype(f32)
    return first, second, rest - second


def row_ids(shape):
    return lax.broadcasted_iota(jnp.int32, shape, 0)


def lane_ids(shape):
    return lax.broadcasted_iota(jnp.int32, shape, 1)


def with_norm(coords):
    norm = jnp.sum(coords * coords, axis=0, keepdims=True)
    return jnp.where(row_ids(coords.shape) == 3, norm, coords), norm


def source_rows(coords):
    value, _ = with_norm(coords)
    one, two, three = split3(value)
    flat = jnp.where(row_ids(value.shape) < 3, f32(1.0), f32(0.0))
    return jnp.concatenate(
        [one, two, three, one, two, one, flat, jnp.zeros_like(one)], axis=0
    ).astype(bf16)


def target_rows(coords):
    value, norm = with_norm(coords)
    one, two, three = split3(value)
    row = row_ids(value.shape)
    main = jnp.where(row < 3, -2.0 * one, jnp.where(row == 3, f32(1.0), f32(0.0)))
    second = jnp.where(row < 3, -2.0 * two, f32(0.0))
    third = jnp.where(row < 3, -2.0 * three, f32(0.0))
    part = split3(norm + soften)
    flat = jnp.where(
        row == 0,
        part[0],
        jnp.where(row == 1, part[1], jnp.where(row == 2, part[2], f32(0.0))),
    )
    return jnp.concatenate(
        [main, main, main, second, second, third, flat, jnp.zeros_like(one)], axis=0
    ).astype(bf16)


def near_counts(nbrs, counts):
    slots, leaves = nbrs.shape
    groups, eight, reach = counts.shape
    span = GROUP + 2 * HL
    rows = -(-span // 16) * 16
    base = nbrs - lane_ids(nbrs.shape) // GROUP * GROUP
    base = jnp.where(nbrs < 0, -1, base)
    ids = row_ids((rows, leaves))
    total = jnp.zeros((rows, leaves), f32)
    for j in range(slots):
        total = total + jnp.where(ids == base[j : j + 1, :], f32(1.0), f32(0.0))
    spread = row_ids((rows, reach)) == lane_ids((rows, reach)) // NPT
    full = lax.dot_general(
        total.T.astype(bf16),
        jnp.where(spread, f32(1.0), f32(0.0)).astype(bf16),
        (((1,), (0,)), ((), ())),
        preferred_element_type=f32,
    )
    counts[...] = full.reshape(groups, eight, reach)


def near_group(g, sources, targets, charges, counts, out):
    reach = counts.shape[2]
    size = GROUP * NPT
    rows = Q * GROUP
    start = pl.multiple_of(g * size, size)
    right = targets[:, pl.ds(start, size)]
    cnt = counts[g]
    ch = charges[:, pl.ds(start, reach)]
    w = jnp.concatenate([cnt * ch[q : q + 1] for q in range(Q)], axis=0)
    wh = w.astype(bf16)
    wl = (w - wh.astype(f32)).astype(bf16)
    w = jnp.concatenate([wh, wl], axis=0)
    total = jnp.zeros((2 * rows, size), f32)
    for at in range(0, reach, 256):
        width = min(256, reach - at)
        left = sources[pl.ds(pl.multiple_of(start + at, size), width), :]
        kernel = lax.rsqrt(jnp.dot(left, right, preferred_element_type=f32))
        high = kernel.astype(bf16)
        low = (kernel - high.astype(f32)).astype(bf16)
        span = slice(at, at + width)
        total = total + jnp.dot(w[:, span], high, preferred_element_type=f32)
        total = total + jnp.dot(w[:, span], low, preferred_element_type=f32)
    flat = total[:rows] + total[rows:]
    mine = row_ids(flat.shape) % GROUP == lane_ids(flat.shape) // NPT
    flat = jnp.where(mine, flat, f32(0.0))
    out[:, pl.ds(start, size)] = jnp.sum(flat.reshape(Q, GROUP, size), axis=1)


def alive_lanes(live, slots, shape):
    slot = lane_ids(shape) // Q
    lower = live // 2
    return (slot < lower) | (slot >= slots - (live - lower))


def m2l_gather(window, lists, gathered):
    offsets, slots = lists.shape
    surface = window.shape[0]
    wide = slots * Q
    expand = row_ids((slots, wide)) == lane_ids((slots, wide)) // Q
    place = jnp.dot(
        (lists + 1).astype(f32).astype(bf16),
        jnp.where(expand, f32(1.0), f32(0.0)).astype(bf16),
        preferred_element_type=f32,
    ).astype(jnp.int32)
    place = (place - 1) * Q + lane_ids(place.shape) % Q
    size = BLOCK * Q
    depth = (BLOCK + slots // 8) * Q
    for b in range(slots // BLOCK):
        block = window[:, b * size : b * size + depth]
        ids = row_ids((depth, size)) + b * size
        for o in range(0, offsets, 2):
            hits = [
                ids == place[k : k + 1, b * size : (b + 1) * size] for k in (o, o + 1)
            ]
            hot = jnp.concatenate([jnp.where(hit, f32(1.0), f32(0.0)) for hit in hits], axis=1)
            pair = jnp.dot(block, hot.astype(bf16), preferred_element_type=f32)
            both = jnp.concatenate([pair[:, :size], pair[:, size:]], axis=0).astype(bf16)
            gathered[o * surface : (o + 2) * surface, b * size : (b + 1) * size] = both


def partial_sums(child, users, send, nx, ny):
    own = SH_DEV * Q
    rows = send.shape[0]
    chunks, count = users.shape
    wide = count * Q
    row = row_ids((rows, wide))
    owner = row // own % nx * ny + row // (own * nx)
    target = owner * own + row % own
    expand = row_ids((count, wide)) == lane_ids((count, wide)) // Q
    expand = jnp.where(expand, f32(1.0), f32(0.0)).astype(bf16)

    def chunk_sum(i):
        ids = users[pl.ds(i, 1), :]
        both = jnp.concatenate([ids // 256, ids % 256], axis=0)
        both = jnp.concatenate([both, both, both, both], axis=0)
        place = jnp.dot(
            both.astype(f32).astype(bf16), expand, preferred_element_type=f32
        ).astype(jnp.int32)
        place = (place[0:1] * 256 + place[1:2]) * Q + lane_ids((1, wide)) % Q
        hot = jnp.where(target == place, f32(1.0), f32(0.0)).astype(bf16)
        block = child[:, pl.ds(pl.multiple_of(i * wide, wide), wide)]
        return lax.dot_general(
            hot, block, (((1,), (1,)), ((), ())), preferred_element_type=f32
        )

    send[...] = chunk_sum(0)
    if chunks > 1:

        def step(i, carry):
            send[...] += chunk_sum(i)
            return carry

        lax.fori_loop(1, chunks, step, 0)


def fused_kernel(
    nx,
    ny,
    live,
    child,
    users,
    local,
    pos,
    charge,
    nbrs,
    window,
    out,
    send1,
    recv1,
    send2,
    recv2,
    spread,
    first,
    last,
    low,
    high,
    pos_low,
    pos_high,
    charge_low,
    charge_high,
    coords,
    charges,
    sources,
    targets,
    counts,
    send_sem,
    recv_sem,
):
    mx, my = lax.axis_index("gx"), lax.axis_index("gy")
    total = nx * ny
    me = mx * ny + my
    after, before = lax.rem(me + 1, total), lax.rem(me + total - 1, total)
    after = (after // ny, lax.rem(after, ny))
    before = (before // ny, lax.rem(before, ny))
    along_y = [(mx, lax.rem(my + d, ny)) for d in range(1, ny)]
    along_x = [(lax.rem(mx + d, nx), my) for d in range(1, nx)]

    barrier = pltpu.get_barrier_semaphore()
    for device in along_y + along_x + [after, before]:
        pl.semaphore_signal(barrier, inc=1, device_id=device, device_id_type=MESH)

    surface, wide = local.shape
    slots = wide // Q
    rim = low.shape[1]
    halo = pos_low.shape[1]
    count = pos.shape[1]
    own = SH_DEV * Q
    message = nx * own
    partial_sums(child, users, send1, nx, ny)
    alive = alive_lanes(live[0], slots, (surface, wide))
    owned = jnp.where(alive, local[...].astype(f32), f32(0.0)).astype(bf16)
    last[...] = owned[:, wide - rim :]
    pl.semaphore_wait(barrier, len(along_y) + len(along_x) + 2)

    at = [0]

    def remote(src, dst, device):
        k = at[0]
        at[0] += 1
        copy = pltpu.make_async_remote_copy(
            src_ref=src,
            dst_ref=dst,
            send_sem=send_sem.at[k],
            recv_sem=recv_sem.at[k],
            device_id=device,
            device_id_type=MESH,
        )
        copy.start()
        return copy

    step1 = []
    for d in range(1, ny):
        start = pl.multiple_of(lax.rem(my + d, ny) * message, message)
        step1.append(
            remote(send1.at[pl.ds(start, message), :], recv1.at[d - 1], along_y[d - 1])
        )
    leaf = [
        remote(pos.at[:, count - halo : count], pos_low, after),
        remote(charge.at[:, count - halo : count], charge_low, after),
        remote(pos.at[:, 0:halo], pos_high, before),
        remote(charge.at[:, 0:halo], charge_high, before),
    ]
    rims = [remote(last, low, after)]

    coords[...] = jnp.zeros_like(coords)
    coords[0:3, halo : halo + count] = pos[...]
    charges[:, halo : halo + count] = charge[...]
    mine = coords[:, halo : halo + count]
    sources[halo : halo + count, :] = source_rows(mine).T
    targets[...] = target_rows(mine)
    near_counts(nbrs[...], counts)
    groups = counts.shape[0]
    skip = halo // (GROUP * NPT)

    def step(g, carry):
        near_group(g, sources, targets, charges, counts, out)
        return carry

    third = (groups - 2 * skip) // 3
    lax.fori_loop(skip, skip + third, step, 0, unroll=2)

    for copy in step1:
        copy.wait()
    value = send1[pl.ds(pl.multiple_of(my * message, message), message), :]
    for d in range(ny - 1):
        value = value + recv1[d]
    for k in range(nx):
        send2[k] = value[k * own : (k + 1) * own]
    step2 = []
    for d in range(1, nx):
        step2.append(remote(send2.at[lax.rem(mx + d, nx)], recv2.at[d - 1], along_x[d - 1]))

    lax.fori_loop(skip + third, skip + 2 * third, step, 0, unroll=2)

    for copy in step2:
        copy.wait()
    shared = send2[mx]
    for d in range(nx - 1):
        shared = shared + recv2[d]
    spread[...] = jnp.zeros_like(spread)
    spread[0:own, :] = shared
    lanes = spread.shape[0]
    front = local[:, 0:lanes].astype(f32) + spread[...].T
    front = jnp.where(alive[:, 0:lanes], front, f32(0.0)).astype(bf16)
    first[...] = front[:, 0:rim]
    rims.append(remote(first, high, before))
    window[:, rim : rim + lanes] = front
    window[:, rim + lanes : rim + wide] = owned[:, lanes:]

    lax.fori_loop(skip + 2 * third, groups - skip, step, 0, unroll=2)

    for copy in leaf:
        copy.wait()
    has_low = me > 0
    has_high = me < total - 1
    for pos_ref, charge_ref, start, there in (
        (pos_low, charge_low, 0, has_low),
        (pos_high, charge_high, halo + count, has_high),
    ):
        span = slice(start, start + halo)
        coords[0:3, span] = pos_ref[...]
        charges[:, span] = jnp.where(there, charge_ref[...], f32(0.0))
        sources[span, :] = source_rows(coords[:, span]).T
    lax.fori_loop(0, skip, step, 0, unroll=2)
    lax.fori_loop(groups - skip, groups, step, 0, unroll=2)

    for copy in rims:
        copy.wait()
    window[:, 0:rim] = jnp.where(has_low, low[...], jnp.zeros_like(low))
    window[:, rim + wide :] = jnp.where(has_high, high[...], jnp.zeros_like(high))


def fused(live, child, users, local, pos, charge, nbrs):
    nx, ny = lax.axis_size("gx"), lax.axis_size("gy")
    surface, wide = local.shape
    count = pos.shape[1]
    halo = HL * NPT
    groups = count // NPT // GROUP
    span = count + 2 * halo
    reach = (GROUP + 2 * HL) * NPT
    rim = wide // 16
    own = SH_DEV * Q
    copies = ny - 1 + nx - 1 + 6
    vmem = pl.BlockSpec(memory_space=pltpu.VMEM)
    return pl.pallas_call(
        functools.partial(fused_kernel, nx, ny),
        out_shape=(
            jax.ShapeDtypeStruct((surface, wide + 2 * rim), bf16),
            jax.ShapeDtypeStruct(charge.shape, f32),
        ),
        in_specs=[pl.BlockSpec(memory_space=pltpu.SMEM)] + [vmem] * 6,
        out_specs=(vmem, vmem),
        scratch_shapes=[
            pltpu.VMEM((ny * nx * own, surface), f32),
            pltpu.VMEM((ny - 1, nx * own, surface), f32),
            pltpu.VMEM((nx, own, surface), f32),
            pltpu.VMEM((nx - 1, own, surface), f32),
            pltpu.VMEM((128, surface), f32),
            pltpu.VMEM((surface, rim), bf16),
            pltpu.VMEM((surface, rim), bf16),
            pltpu.VMEM((surface, rim), bf16),
            pltpu.VMEM((surface, rim), bf16),
            pltpu.VMEM((3, halo), f32),
            pltpu.VMEM((3, halo), f32),
            pltpu.VMEM((Q, halo), f32),
            pltpu.VMEM((Q, halo), f32),
            pltpu.VMEM((8, span), f32),
            pltpu.VMEM((Q, span), f32),
            pltpu.VMEM((span, 64), bf16),
            pltpu.VMEM((64, count), bf16),
            pltpu.VMEM((groups, GROUP, reach), f32),
            pltpu.SemaphoreType.DMA((copies,)),
            pltpu.SemaphoreType.DMA((copies,)),
        ],
        compiler_params=pltpu.CompilerParams(collective_id=0, has_side_effects=True),
    )(live, child, users.reshape(-1, 64), local, pos, charge, nbrs.T)


def m2l_kernel(live, window, lists, ops, near, out, near_out, gathered, held, sem):
    fetch = pltpu.make_async_copy(ops, held, sem)
    fetch.start()
    near_out[...] = near[...]
    m2l_gather(window, lists[...], gathered)
    fetch.wait()
    result = jnp.dot(held[...], gathered[...], preferred_element_type=f32)
    alive = alive_lanes(live[0], lists.shape[1], result.shape)
    out[...] = jnp.where(alive, result, f32(0.0))


def m2l(live, window, lists, ops, near):
    surface = window.shape[0]
    wide = lists.shape[1] * Q
    vmem = pl.BlockSpec(memory_space=pltpu.VMEM)
    return pl.pallas_call(
        m2l_kernel,
        out_shape=(
            jax.ShapeDtypeStruct((surface, wide), f32),
            jax.ShapeDtypeStruct(near.shape, f32),
        ),
        in_specs=[pl.BlockSpec(memory_space=pltpu.SMEM)] + [vmem] * 2
        + [pl.BlockSpec(memory_space=pl.ANY), vmem],
        out_specs=(vmem, vmem),
        scratch_shapes=[
            pltpu.VMEM((surface * lists.shape[0], wide), bf16),
            pltpu.VMEM(ops.shape, bf16),
            pltpu.SemaphoreType.DMA,
        ],
    )(live, window, lists, ops, near)


def per_device(
    child_dens, users, local_dens, live, m2l_ops, m2l_lists, leaf_pos, leaf_charge, leaf_nbrs
):
    window, near_pot = fused(
        live, child_dens, users, local_dens, leaf_pos, leaf_charge, leaf_nbrs
    )
    return m2l(live, window, m2l_lists, m2l_ops, near_pot)


def solution(mesh):
    placed = (
        P(None, ("gx", "gy")),
        P(("gx", "gy")),
        P(None, ("gx", "gy")),
        P(("gx", "gy")),
        P(),
        P(None, ("gx", "gy")),
        P(None, ("gx", "gy")),
        P(None, ("gx", "gy")),
        P(("gx", "gy"), None),
    )
    return jax.shard_map(
        per_device,
        mesh=mesh,
        in_specs=placed,
        out_specs=(P(None, ("gx", "gy")), P(None, ("gx", "gy"))),
        check_vma=False,
    )
```

```python
import functools

import jax
import jax.numpy as jnp
from jax import lax
from jax.experimental import pallas as pl
from jax.experimental.pallas import tpu as pltpu
from jax.sharding import PartitionSpec as P

Q = 4
NOFF = 8
SH_DEV = 1
NPT = 32
HL = 16
GROUP = 8
BLOCK = 32

soften = 0.01
f32 = jnp.float32
bf16 = jnp.bfloat16
MESH = pl.DeviceIdType.MESH


def split3(value):
    first = value.astype(bf16).astype(f32)
    rest = value - first
    second = rest.astype(bf16).astype(f32)
    return first, second, rest - second


def row_ids(shape):
    return lax.broadcasted_iota(jnp.int32, shape, 0)


def lane_ids(shape):
    return lax.broadcasted_iota(jnp.int32, shape, 1)


def with_norm(coords):
    norm = jnp.sum(coords * coords, axis=0, keepdims=True)
    return jnp.where(row_ids(coords.shape) == 3, norm, coords), norm


def source_rows(coords):
    value, _ = with_norm(coords)
    one, two, three = split3(value)
    flat = jnp.where(row_ids(value.shape) < 3, f32(1.0), f32(0.0))
    return jnp.concatenate(
        [one, two, three, one, two, one, flat, jnp.zeros_like(one)], axis=0
    ).astype(bf16)


def target_rows(coords):
    value, norm = with_norm(coords)
    one, two, three = split3(value)
    row = row_ids(value.shape)
    main = jnp.where(row < 3, -2.0 * one, jnp.where(row == 3, f32(1.0), f32(0.0)))
    second = jnp.where(row < 3, -2.0 * two, f32(0.0))
    third = jnp.where(row < 3, -2.0 * three, f32(0.0))
    part = split3(norm + soften)
    flat = jnp.where(
        row == 0,
        part[0],
        jnp.where(row == 1, part[1], jnp.where(row == 2, part[2], f32(0.0))),
    )
    return jnp.concatenate(
        [main, main, main, second, second, third, flat, jnp.zeros_like(one)], axis=0
    ).astype(bf16)


def near_counts(nbrs, counts):
    slots, leaves = nbrs.shape
    groups, eight, reach = counts.shape
    span = GROUP + 2 * HL
    rows = -(-span // 16) * 16
    base = nbrs - lane_ids(nbrs.shape) // GROUP * GROUP
    base = jnp.where(nbrs < 0, -1, base)
    ids = row_ids((rows, leaves))
    total = jnp.zeros((rows, leaves), f32)
    for j in range(slots):
        total = total + jnp.where(ids == base[j : j + 1, :], f32(1.0), f32(0.0))
    spread = row_ids((rows, reach)) == lane_ids((rows, reach)) // NPT
    full = lax.dot_general(
        total.T.astype(bf16),
        jnp.where(spread, f32(1.0), f32(0.0)).astype(bf16),
        (((1,), (0,)), ((), ())),
        preferred_element_type=f32,
    )
    counts[...] = full.reshape(groups, eight, reach)


def near_group(g, sources, targets, charges, counts, out):
    reach = counts.shape[2]
    size = GROUP * NPT
    rows = Q * GROUP
    start = pl.multiple_of(g * size, size)
    right = targets[:, pl.ds(start, size)]
    cnt = counts[g]
    ch = charges[:, pl.ds(start, reach)]
    w = jnp.concatenate([cnt * ch[q : q + 1] for q in range(Q)], axis=0)
    wh = w.astype(bf16)
    wl = (w - wh.astype(f32)).astype(bf16)
    w = jnp.concatenate([wh, wl], axis=0)
    total = jnp.zeros((2 * rows, size), f32)
    for at in range(0, reach, 256):
        width = min(256, reach - at)
        left = sources[pl.ds(pl.multiple_of(start + at, size), width), :]
        kernel = lax.rsqrt(jnp.dot(left, right, preferred_element_type=f32))
        high = kernel.astype(bf16)
        low = (kernel - high.astype(f32)).astype(bf16)
        span = slice(at, at + width)
        total = total + jnp.dot(w[:, span], high, preferred_element_type=f32)
        total = total + jnp.dot(w[:, span], low, preferred_element_type=f32)
    flat = total[:rows] + total[rows:]
    mine = row_ids(flat.shape) % GROUP == lane_ids(flat.shape) // NPT
    flat = jnp.where(mine, flat, f32(0.0))
    out[:, pl.ds(start, size)] = jnp.sum(flat.reshape(Q, GROUP, size), axis=1)


def alive_lanes(live, slots, shape):
    slot = lane_ids(shape) // Q
    lower = live // 2
    return (slot < lower) | (slot >= slots - (live - lower))


def m2l_gather(window, lists, gathered):
    offsets, slots = lists.shape
    surface = window.shape[0]
    wide = slots * Q
    expand = row_ids((slots, wide)) == lane_ids((slots, wide)) // Q
    place = jnp.dot(
        (lists + 1).astype(f32).astype(bf16),
        jnp.where(expand, f32(1.0), f32(0.0)).astype(bf16),
        preferred_element_type=f32,
    ).astype(jnp.int32)
    place = (place - 1) * Q + lane_ids(place.shape) % Q
    size = BLOCK * Q
    depth = (BLOCK + slots // 8) * Q
    for b in range(slots // BLOCK):
        block = window[:, b * size : b * size + depth]
        ids = row_ids((depth, size)) + b * size
        for o in range(0, offsets, 2):
            hits = [
                ids == place[k : k + 1, b * size : (b + 1) * size] for k in (o, o + 1)
            ]
            hot = jnp.concatenate([jnp.where(hit, f32(1.0), f32(0.0)) for hit in hits], axis=1)
            pair = jnp.dot(block, hot.astype(bf16), preferred_element_type=f32)
            both = jnp.concatenate([pair[:, :size], pair[:, size:]], axis=0).astype(bf16)
            gathered[o * surface : (o + 2) * surface, b * size : (b + 1) * size] = both


def partial_sums(child, users, send, nx, ny):
    own = SH_DEV * Q
    rows = send.shape[0]
    chunks, count = users.shape
    wide = count * Q
    row = row_ids((rows, wide))
    owner = row // own % nx * ny + row // (own * nx)
    target = owner * own + row % own
    expand = row_ids((count, wide)) == lane_ids((count, wide)) // Q
    expand = jnp.where(expand, f32(1.0), f32(0.0)).astype(bf16)

    def chunk_sum(i):
        ids = users[pl.ds(i, 1), :]
        both = jnp.concatenate([ids // 256, ids % 256], axis=0)
        both = jnp.concatenate([both, both, both, both], axis=0)
        place = jnp.dot(
            both.astype(f32).astype(bf16), expand, preferred_element_type=f32
        ).astype(jnp.int32)
        place = (place[0:1] * 256 + place[1:2]) * Q + lane_ids((1, wide)) % Q
        hot = jnp.where(target == place, f32(1.0), f32(0.0)).astype(bf16)
        block = child[:, pl.ds(pl.multiple_of(i * wide, wide), wide)]
        return lax.dot_general(
            hot, block, (((1,), (1,)), ((), ())), preferred_element_type=f32
        )

    send[...] = chunk_sum(0)
    if chunks > 1:

        def step(i, carry):
            send[...] += chunk_sum(i)
            return carry

        lax.fori_loop(1, chunks, step, 0)


def fused_kernel(
    nx,
    ny,
    live,
    child,
    users,
    local,
    pos,
    charge,
    nbrs,
    window,
    out,
    send1,
    recv1,
    send2,
    recv2,
    spread,
    first,
    last,
    low,
    high,
    pos_low,
    pos_high,
    charge_low,
    charge_high,
    coords,
    charges,
    sources,
    targets,
    counts,
    send_sem,
    recv_sem,
):
    mx, my = lax.axis_index("gx"), lax.axis_index("gy")
    total = nx * ny
    me = mx * ny + my
    after, before = lax.rem(me + 1, total), lax.rem(me + total - 1, total)
    after = (after // ny, lax.rem(after, ny))
    before = (before // ny, lax.rem(before, ny))
    along_y = [(mx, lax.rem(my + d, ny)) for d in range(1, ny)]
    along_x = [(lax.rem(mx + d, nx), my) for d in range(1, nx)]

    barrier = pltpu.get_barrier_semaphore()
    for device in along_y + along_x + [after, before]:
        pl.semaphore_signal(barrier, inc=1, device_id=device, device_id_type=MESH)

    surface, wide = local.shape
    slots = wide // Q
    rim = low.shape[1]
    halo = pos_low.shape[1]
    count = pos.shape[1]
    own = SH_DEV * Q
    message = nx * own
    partial_sums(child, users, send1, nx, ny)
    alive = alive_lanes(live[0], slots, (surface, wide))
    owned = jnp.where(alive, local[...].astype(f32), f32(0.0)).astype(bf16)
    last[...] = owned[:, wide - rim :]
    pl.semaphore_wait(barrier, len(along_y) + len(along_x) + 2)

    at = [0]

    def remote(src, dst, device):
        k = at[0]
        at[0] += 1
        copy = pltpu.make_async_remote_copy(
            src_ref=src,
            dst_ref=dst,
            send_sem=send_sem.at[k],
            recv_sem=recv_sem.at[k],
            device_id=device,
            device_id_type=MESH,
        )
        copy.start()
        return copy

    step1 = []
    for d in range(1, ny):
        start = pl.multiple_of(lax.rem(my + d, ny) * message, message)
        step1.append(
            remote(send1.at[pl.ds(start, message), :], recv1.at[d - 1], along_y[d - 1])
        )
    leaf = [
        remote(pos.at[:, count - halo : count], pos_low, after),
        remote(charge.at[:, count - halo : count], charge_low, after),
        remote(pos.at[:, 0:halo], pos_high, before),
        remote(charge.at[:, 0:halo], charge_high, before),
    ]
    rims = [remote(last, low, after)]

    coords[...] = jnp.zeros_like(coords)
    coords[0:3, halo : halo + count] = pos[...]
    charges[:, halo : halo + count] = charge[...]
    mine = coords[:, halo : halo + count]
    sources[halo : halo + count, :] = source_rows(mine).T
    targets[...] = target_rows(mine)
    near_counts(nbrs[...], counts)
    groups = counts.shape[0]
    skip = halo // (GROUP * NPT)

    def step(g, carry):
        near_group(g, sources, targets, charges, counts, out)
        return carry

    third = (groups - 2 * skip) // 3
    lax.fori_loop(skip, skip + third, step, 0, unroll=4)

    for copy in step1:
        copy.wait()
    value = send1[pl.ds(pl.multiple_of(my * message, message), message), :]
    for d in range(ny - 1):
        value = value + recv1[d]
    for k in range(nx):
        send2[k] = value[k * own : (k + 1) * own]
    step2 = []
    for d in range(1, nx):
        step2.append(remote(send2.at[lax.rem(mx + d, nx)], recv2.at[d - 1], along_x[d - 1]))

    lax.fori_loop(skip + third, skip + 2 * third, step, 0, unroll=4)

    for copy in step2:
        copy.wait()
    shared = send2[mx]
    for d in range(nx - 1):
        shared = shared + recv2[d]
    spread[...] = jnp.zeros_like(spread)
    spread[0:own, :] = shared
    lanes = spread.shape[0]
    front = local[:, 0:lanes].astype(f32) + spread[...].T
    front = jnp.where(alive[:, 0:lanes], front, f32(0.0)).astype(bf16)
    first[...] = front[:, 0:rim]
    rims.append(remote(first, high, before))
    window[:, rim : rim + lanes] = front
    window[:, rim + lanes : rim + wide] = owned[:, lanes:]

    lax.fori_loop(skip + 2 * third, groups - skip, step, 0, unroll=4)

    for copy in leaf:
        copy.wait()
    has_low = me > 0
    has_high = me < total - 1
    for pos_ref, charge_ref, start, there in (
        (pos_low, charge_low, 0, has_low),
        (pos_high, charge_high, halo + count, has_high),
    ):
        span = slice(start, start + halo)
        coords[0:3, span] = pos_ref[...]
        charges[:, span] = jnp.where(there, charge_ref[...], f32(0.0))
        sources[span, :] = source_rows(coords[:, span]).T
    lax.fori_loop(0, skip, step, 0, unroll=2)
    lax.fori_loop(groups - skip, groups, step, 0, unroll=2)

    for copy in rims:
        copy.wait()
    window[:, 0:rim] = jnp.where(has_low, low[...], jnp.zeros_like(low))
    window[:, rim + wide :] = jnp.where(has_high, high[...], jnp.zeros_like(high))


def fused(live, child, users, local, pos, charge, nbrs):
    nx, ny = lax.axis_size("gx"), lax.axis_size("gy")
    surface, wide = local.shape
    count = pos.shape[1]
    halo = HL * NPT
    groups = count // NPT // GROUP
    span = count + 2 * halo
    reach = (GROUP + 2 * HL) * NPT
    rim = wide // 16
    own = SH_DEV * Q
    copies = ny - 1 + nx - 1 + 6
    vmem = pl.BlockSpec(memory_space=pltpu.VMEM)
    return pl.pallas_call(
        functools.partial(fused_kernel, nx, ny),
        out_shape=(
            jax.ShapeDtypeStruct((surface, wide + 2 * rim), bf16),
            jax.ShapeDtypeStruct(charge.shape, f32),
        ),
        in_specs=[pl.BlockSpec(memory_space=pltpu.SMEM)] + [vmem] * 6,
        out_specs=(vmem, vmem),
        scratch_shapes=[
            pltpu.VMEM((ny * nx * own, surface), f32),
            pltpu.VMEM((ny - 1, nx * own, surface), f32),
            pltpu.VMEM((nx, own, surface), f32),
            pltpu.VMEM((nx - 1, own, surface), f32),
            pltpu.VMEM((128, surface), f32),
            pltpu.VMEM((surface, rim), bf16),
            pltpu.VMEM((surface, rim), bf16),
            pltpu.VMEM((surface, rim), bf16),
            pltpu.VMEM((surface, rim), bf16),
            pltpu.VMEM((3, halo), f32),
            pltpu.VMEM((3, halo), f32),
            pltpu.VMEM((Q, halo), f32),
            pltpu.VMEM((Q, halo), f32),
            pltpu.VMEM((8, span), f32),
            pltpu.VMEM((Q, span), f32),
            pltpu.VMEM((span, 64), bf16),
            pltpu.VMEM((64, count), bf16),
            pltpu.VMEM((groups, GROUP, reach), f32),
            pltpu.SemaphoreType.DMA((copies,)),
            pltpu.SemaphoreType.DMA((copies,)),
        ],
        compiler_params=pltpu.CompilerParams(collective_id=0, has_side_effects=True),
    )(live, child, users.reshape(-1, 64), local, pos, charge, nbrs.T)


def m2l_kernel(live, window, lists, ops, near, out, near_out, gathered, held, sem):
    fetch = pltpu.make_async_copy(ops, held, sem)
    fetch.start()
    near_out[...] = near[...]
    m2l_gather(window, lists[...], gathered)
    fetch.wait()
    result = jnp.dot(held[...], gathered[...], preferred_element_type=f32)
    alive = alive_lanes(live[0], lists.shape[1], result.shape)
    out[...] = jnp.where(alive, result, f32(0.0))


def m2l(live, window, lists, ops, near):
    surface = window.shape[0]
    wide = lists.shape[1] * Q
    vmem = pl.BlockSpec(memory_space=pltpu.VMEM)
    return pl.pallas_call(
        m2l_kernel,
        out_shape=(
            jax.ShapeDtypeStruct((surface, wide), f32),
            jax.ShapeDtypeStruct(near.shape, f32),
        ),
        in_specs=[pl.BlockSpec(memory_space=pltpu.SMEM)] + [vmem] * 2
        + [pl.BlockSpec(memory_space=pl.ANY), vmem],
        out_specs=(vmem, vmem),
        scratch_shapes=[
            pltpu.VMEM((surface * lists.shape[0], wide), bf16),
            pltpu.VMEM(ops.shape, bf16),
            pltpu.SemaphoreType.DMA,
        ],
    )(live, window, lists, ops, near)


def per_device(
    child_dens, users, local_dens, live, m2l_ops, m2l_lists, leaf_pos, leaf_charge, leaf_nbrs
):
    window, near_pot = fused(
        live, child_dens, users, local_dens, leaf_pos, leaf_charge, leaf_nbrs
    )
    return m2l(live, window, m2l_lists, m2l_ops, near_pot)


def solution(mesh):
    placed = (
        P(None, ("gx", "gy")),
        P(("gx", "gy")),
        P(None, ("gx", "gy")),
        P(("gx", "gy")),
        P(),
        P(None, ("gx", "gy")),
        P(None, ("gx", "gy")),
        P(None, ("gx", "gy")),
        P(("gx", "gy"), None),
    )
    return jax.shard_map(
        per_device,
        mesh=mesh,
        in_specs=placed,
        out_specs=(P(None, ("gx", "gy")), P(None, ("gx", "gy"))),
        check_vma=False,
    )
```

```python
import functools

import jax
import jax.numpy as jnp
from jax import lax
from jax.experimental import pallas as pl
from jax.experimental.pallas import tpu as pltpu
from jax.sharding import PartitionSpec as P

Q = 4
NOFF = 8
SH_DEV = 1
NPT = 32
HL = 16
GROUP = 8
BLOCK = 32

soften = 0.01
f32 = jnp.float32
bf16 = jnp.bfloat16
MESH = pl.DeviceIdType.MESH


def split3(value):
    first = value.astype(bf16).astype(f32)
    rest = value - first
    second = rest.astype(bf16).astype(f32)
    return first, second, rest - second


def row_ids(shape):
    return lax.broadcasted_iota(jnp.int32, shape, 0)


def lane_ids(shape):
    return lax.broadcasted_iota(jnp.int32, shape, 1)


def with_norm(coords):
    norm = jnp.sum(coords * coords, axis=0, keepdims=True)
    return jnp.where(row_ids(coords.shape) == 3, norm, coords), norm


def source_rows(coords):
    value, _ = with_norm(coords)
    one, two, three = split3(value)
    flat = jnp.where(row_ids(value.shape) < 3, f32(1.0), f32(0.0))
    return jnp.concatenate(
        [one, two, three, one, two, one, flat, jnp.zeros_like(one)], axis=0
    ).astype(bf16)


def target_rows(coords):
    value, norm = with_norm(coords)
    one, two, three = split3(value)
    row = row_ids(value.shape)
    main = jnp.where(row < 3, -2.0 * one, jnp.where(row == 3, f32(1.0), f32(0.0)))
    second = jnp.where(row < 3, -2.0 * two, f32(0.0))
    third = jnp.where(row < 3, -2.0 * three, f32(0.0))
    part = split3(norm + soften)
    flat = jnp.where(
        row == 0,
        part[0],
        jnp.where(row == 1, part[1], jnp.where(row == 2, part[2], f32(0.0))),
    )
    return jnp.concatenate(
        [main, main, main, second, second, third, flat, jnp.zeros_like(one)], axis=0
    ).astype(bf16)


def near_counts(nbrs, counts):
    slots, leaves = nbrs.shape
    groups, eight, reach = counts.shape
    span = GROUP + 2 * HL
    rows = -(-span // 16) * 16
    base = nbrs - lane_ids(nbrs.shape) // GROUP * GROUP
    base = jnp.where(nbrs < 0, -1, base)
    ids = row_ids((rows, leaves))
    total = jnp.zeros((rows, leaves), f32)
    for j in range(slots):
        total = total + jnp.where(ids == base[j : j + 1, :], f32(1.0), f32(0.0))
    spread = row_ids((rows, reach)) == lane_ids((rows, reach)) // NPT
    full = lax.dot_general(
        total.T.astype(bf16),
        jnp.where(spread, f32(1.0), f32(0.0)).astype(bf16),
        (((1,), (0,)), ((), ())),
        preferred_element_type=f32,
    )
    counts[...] = full.reshape(groups, eight, reach)


def near_group(g, sources, targets, charges, counts, out):
    reach = counts.shape[2]
    size = GROUP * NPT
    rows = Q * GROUP
    start = pl.multiple_of(g * size, size)
    right = targets[:, pl.ds(start, size)]
    cnt = counts[g]
    ch = charges[:, pl.ds(start, reach)]
    w = jnp.concatenate([cnt * ch[q : q + 1] for q in range(Q)], axis=0)
    wh = w.astype(bf16)
    wl = (w - wh.astype(f32)).astype(bf16)
    w = jnp.concatenate([wh, wl], axis=0)
    total = jnp.zeros((2 * rows, size), f32)
    for at in range(0, reach, 256):
        width = min(256, reach - at)
        left = sources[pl.ds(pl.multiple_of(start + at, size), width), :]
        kernel = lax.rsqrt(jnp.dot(left, right, preferred_element_type=f32))
        high = kernel.astype(bf16)
        low = (kernel - high.astype(f32)).astype(bf16)
        span = slice(at, at + width)
        total = total + jnp.dot(w[:, span], high, preferred_element_type=f32)
        total = total + jnp.dot(w[:, span], low, preferred_element_type=f32)
    flat = total[:rows] + total[rows:]
    mine = row_ids(flat.shape) % GROUP == lane_ids(flat.shape) // NPT
    flat = jnp.where(mine, flat, f32(0.0))
    out[:, pl.ds(start, size)] = jnp.sum(flat.reshape(Q, GROUP, size), axis=1)


def alive_lanes(live, slots, shape):
    slot = lane_ids(shape) // Q
    lower = live // 2
    return (slot < lower) | (slot >= slots - (live - lower))


def m2l_gather(window, lists, gathered, ready):
    offsets, slots = lists.shape
    surface = window.shape[0]
    wide = slots * Q
    expand = row_ids((slots, wide)) == lane_ids((slots, wide)) // Q
    place = jnp.dot(
        (lists + 1).astype(f32).astype(bf16),
        jnp.where(expand, f32(1.0), f32(0.0)).astype(bf16),
        preferred_element_type=f32,
    ).astype(jnp.int32)
    place = (place - 1) * Q + lane_ids(place.shape) % Q
    size = BLOCK * Q
    depth = (BLOCK + slots // 8) * Q
    for b in range(slots // BLOCK):
        block = window[:, b * size : b * size + depth]
        ids = row_ids((depth, size)) + b * size
        for o in range(0, offsets, 2):
            hits = [
                ids == place[k : k + 1, b * size : (b + 1) * size] for k in (o, o + 1)
            ]
            hot = jnp.concatenate([jnp.where(hit, f32(1.0), f32(0.0)) for hit in hits], axis=1)
            pair = jnp.dot(block, hot.astype(bf16), preferred_element_type=f32)
            both = jnp.concatenate([pair[:, :size], pair[:, size:]], axis=0).astype(bf16)
            gathered[o * surface : (o + 2) * surface, b * size : (b + 1) * size] = both
        if b % 2 == 1:
            ready((b - 1) * size, 2 * size)


def partial_sums(child, users, send, nx, ny):
    own = SH_DEV * Q
    rows = send.shape[0]
    chunks, count = users.shape
    wide = count * Q
    row = row_ids((rows, wide))
    owner = row // own % nx * ny + row // (own * nx)
    target = owner * own + row % own
    expand = row_ids((count, wide)) == lane_ids((count, wide)) // Q
    expand = jnp.where(expand, f32(1.0), f32(0.0)).astype(bf16)

    def chunk_sum(i):
        ids = users[pl.ds(i, 1), :]
        both = jnp.concatenate([ids // 256, ids % 256], axis=0)
        both = jnp.concatenate([both, both, both, both], axis=0)
        place = jnp.dot(
            both.astype(f32).astype(bf16), expand, preferred_element_type=f32
        ).astype(jnp.int32)
        place = (place[0:1] * 256 + place[1:2]) * Q + lane_ids((1, wide)) % Q
        hot = jnp.where(target == place, f32(1.0), f32(0.0)).astype(bf16)
        block = child[:, pl.ds(pl.multiple_of(i * wide, wide), wide)]
        return lax.dot_general(
            hot, block, (((1,), (1,)), ((), ())), preferred_element_type=f32
        )

    send[...] = chunk_sum(0)
    if chunks > 1:

        def step(i, carry):
            send[...] += chunk_sum(i)
            return carry

        lax.fori_loop(1, chunks, step, 0)


def fused_kernel(
    nx,
    ny,
    live,
    child,
    users,
    local,
    pos,
    charge,
    nbrs,
    window,
    out,
    send1,
    recv1,
    send2,
    recv2,
    spread,
    first,
    last,
    low,
    high,
    pos_low,
    pos_high,
    charge_low,
    charge_high,
    coords,
    charges,
    sources,
    targets,
    counts,
    send_sem,
    recv_sem,
):
    mx, my = lax.axis_index("gx"), lax.axis_index("gy")
    total = nx * ny
    me = mx * ny + my
    after, before = lax.rem(me + 1, total), lax.rem(me + total - 1, total)
    after = (after // ny, lax.rem(after, ny))
    before = (before // ny, lax.rem(before, ny))
    along_y = [(mx, lax.rem(my + d, ny)) for d in range(1, ny)]
    along_x = [(lax.rem(mx + d, nx), my) for d in range(1, nx)]

    barrier = pltpu.get_barrier_semaphore()
    for device in along_y + along_x + [after, before]:
        pl.semaphore_signal(barrier, inc=1, device_id=device, device_id_type=MESH)

    surface, wide = local.shape
    slots = wide // Q
    rim = low.shape[1]
    halo = pos_low.shape[1]
    count = pos.shape[1]
    own = SH_DEV * Q
    message = nx * own
    partial_sums(child, users, send1, nx, ny)
    alive = alive_lanes(live[0], slots, (surface, wide))
    owned = jnp.where(alive, local[...].astype(f32), f32(0.0)).astype(bf16)
    last[...] = owned[:, wide - rim :]
    pl.semaphore_wait(barrier, len(along_y) + len(along_x) + 2)

    at = [0]

    def remote(src, dst, device):
        k = at[0]
        at[0] += 1
        copy = pltpu.make_async_remote_copy(
            src_ref=src,
            dst_ref=dst,
            send_sem=send_sem.at[k],
            recv_sem=recv_sem.at[k],
            device_id=device,
            device_id_type=MESH,
        )
        copy.start()
        return copy

    step1 = []
    for d in range(1, ny):
        start = pl.multiple_of(lax.rem(my + d, ny) * message, message)
        step1.append(
            remote(send1.at[pl.ds(start, message), :], recv1.at[d - 1], along_y[d - 1])
        )
    leaf = [
        remote(pos.at[:, count - halo : count], pos_low, after),
        remote(charge.at[:, count - halo : count], charge_low, after),
        remote(pos.at[:, 0:halo], pos_high, before),
        remote(charge.at[:, 0:halo], charge_high, before),
    ]
    rims = [remote(last, low, after)]

    coords[...] = jnp.zeros_like(coords)
    coords[0:3, halo : halo + count] = pos[...]
    charges[:, halo : halo + count] = charge[...]
    mine = coords[:, halo : halo + count]
    sources[halo : halo + count, :] = source_rows(mine).T
    targets[...] = target_rows(mine)
    near_counts(nbrs[...], counts)
    groups = counts.shape[0]
    skip = halo // (GROUP * NPT)

    def step(g, carry):
        near_group(g, sources, targets, charges, counts, out)
        return carry

    third = (groups - 2 * skip) // 3
    lax.fori_loop(skip, skip + third, step, 0, unroll=4)

    for copy in step1:
        copy.wait()
    value = send1[pl.ds(pl.multiple_of(my * message, message), message), :]
    for d in range(ny - 1):
        value = value + recv1[d]
    for k in range(nx):
        send2[k] = value[k * own : (k + 1) * own]
    step2 = []
    for d in range(1, nx):
        step2.append(remote(send2.at[lax.rem(mx + d, nx)], recv2.at[d - 1], along_x[d - 1]))

    lax.fori_loop(skip + third, skip + 2 * third, step, 0, unroll=4)

    for copy in step2:
        copy.wait()
    shared = send2[mx]
    for d in range(nx - 1):
        shared = shared + recv2[d]
    spread[...] = jnp.zeros_like(spread)
    spread[0:own, :] = shared
    lanes = spread.shape[0]
    front = local[:, 0:lanes].astype(f32) + spread[...].T
    front = jnp.where(alive[:, 0:lanes], front, f32(0.0)).astype(bf16)
    first[...] = front[:, 0:rim]
    rims.append(remote(first, high, before))
    window[:, rim : rim + lanes] = front
    window[:, rim + lanes : rim + wide] = owned[:, lanes:]

    lax.fori_loop(skip + 2 * third, groups - skip, step, 0, unroll=4)

    for copy in leaf:
        copy.wait()
    has_low = me > 0
    has_high = me < total - 1
    for pos_ref, charge_ref, start, there in (
        (pos_low, charge_low, 0, has_low),
        (pos_high, charge_high, halo + count, has_high),
    ):
        span = slice(start, start + halo)
        coords[0:3, span] = pos_ref[...]
        charges[:, span] = jnp.where(there, charge_ref[...], f32(0.0))
        sources[span, :] = source_rows(coords[:, span]).T
    lax.fori_loop(0, skip, step, 0, unroll=2)
    lax.fori_loop(groups - skip, groups, step, 0, unroll=2)

    for copy in rims:
        copy.wait()
    window[:, 0:rim] = jnp.where(has_low, low[...], jnp.zeros_like(low))
    window[:, rim + wide :] = jnp.where(has_high, high[...], jnp.zeros_like(high))


def fused(live, child, users, local, pos, charge, nbrs):
    nx, ny = lax.axis_size("gx"), lax.axis_size("gy")
    surface, wide = local.shape
    count = pos.shape[1]
    halo = HL * NPT
    groups = count // NPT // GROUP
    span = count + 2 * halo
    reach = (GROUP + 2 * HL) * NPT
    rim = wide // 16
    own = SH_DEV * Q
    copies = ny - 1 + nx - 1 + 6
    vmem = pl.BlockSpec(memory_space=pltpu.VMEM)
    return pl.pallas_call(
        functools.partial(fused_kernel, nx, ny),
        out_shape=(
            jax.ShapeDtypeStruct((surface, wide + 2 * rim), bf16),
            jax.ShapeDtypeStruct(charge.shape, f32),
        ),
        in_specs=[pl.BlockSpec(memory_space=pltpu.SMEM)] + [vmem] * 6,
        out_specs=(vmem, vmem),
        scratch_shapes=[
            pltpu.VMEM((ny * nx * own, surface), f32),
            pltpu.VMEM((ny - 1, nx * own, surface), f32),
            pltpu.VMEM((nx, own, surface), f32),
            pltpu.VMEM((nx - 1, own, surface), f32),
            pltpu.VMEM((128, surface), f32),
            pltpu.VMEM((surface, rim), bf16),
            pltpu.VMEM((surface, rim), bf16),
            pltpu.VMEM((surface, rim), bf16),
            pltpu.VMEM((surface, rim), bf16),
            pltpu.VMEM((3, halo), f32),
            pltpu.VMEM((3, halo), f32),
            pltpu.VMEM((Q, halo), f32),
            pltpu.VMEM((Q, halo), f32),
            pltpu.VMEM((8, span), f32),
            pltpu.VMEM((Q, span), f32),
            pltpu.VMEM((span, 64), bf16),
            pltpu.VMEM((64, count), bf16),
            pltpu.VMEM((groups, GROUP, reach), f32),
            pltpu.SemaphoreType.DMA((copies,)),
            pltpu.SemaphoreType.DMA((copies,)),
        ],
        compiler_params=pltpu.CompilerParams(collective_id=0, has_side_effects=True),
    )(live, child, users.reshape(-1, 64), local, pos, charge, nbrs.T)


def m2l_kernel(live, window, lists, ops, near, out, near_out, gathered, held, staged, sem, out_sem):
    fetch = pltpu.make_async_copy(ops, held, sem)
    fetch.start()
    near_out[...] = near[...]
    copies = []

    def ready(start, size):
        if start == 0:
            fetch.wait()
        span = slice(start, start + size)
        result = jnp.dot(held[...], gathered[:, span], preferred_element_type=f32)
        alive = alive_lanes(live[0], lists.shape[1], staged.shape)[:, span]
        staged[:, span] = jnp.where(alive, result, f32(0.0))
        copies.append(
            pltpu.make_async_copy(staged.at[:, span], out.at[:, span], out_sem.at[len(copies)])
        )
        copies[-1].start()

    m2l_gather(window, lists[...], gathered, ready)
    for copy in copies:
        copy.wait()


def m2l(live, window, lists, ops, near):
    surface = window.shape[0]
    wide = lists.shape[1] * Q
    vmem = pl.BlockSpec(memory_space=pltpu.VMEM)
    return pl.pallas_call(
        m2l_kernel,
        out_shape=(
            jax.ShapeDtypeStruct((surface, wide), f32),
            jax.ShapeDtypeStruct(near.shape, f32),
        ),
        in_specs=[pl.BlockSpec(memory_space=pltpu.SMEM)] + [vmem] * 2
        + [pl.BlockSpec(memory_space=pl.ANY), vmem],
        out_specs=(pl.BlockSpec(memory_space=pl.ANY), vmem),
        scratch_shapes=[
            pltpu.VMEM((surface * lists.shape[0], wide), bf16),
            pltpu.VMEM(ops.shape, bf16),
            pltpu.VMEM((surface, wide), f32),
            pltpu.SemaphoreType.DMA,
            pltpu.SemaphoreType.DMA((wide // (2 * BLOCK * Q),)),
        ],
    )(live, window, lists, ops, near)


def per_device(
    child_dens, users, local_dens, live, m2l_ops, m2l_lists, leaf_pos, leaf_charge, leaf_nbrs
):
    window, near_pot = fused(
        live, child_dens, users, local_dens, leaf_pos, leaf_charge, leaf_nbrs
    )
    return m2l(live, window, m2l_lists, m2l_ops, near_pot)


def solution(mesh):
    placed = (
        P(None, ("gx", "gy")),
        P(("gx", "gy")),
        P(None, ("gx", "gy")),
        P(("gx", "gy")),
        P(),
        P(None, ("gx", "gy")),
        P(None, ("gx", "gy")),
        P(None, ("gx", "gy")),
        P(("gx", "gy"), None),
    )
    return jax.shard_map(
        per_device,
        mesh=mesh,
        in_specs=placed,
        out_specs=(P(None, ("gx", "gy")), P(None, ("gx", "gy"))),
        check_vma=False,
    )
```
